32 devices in a mesh: row: 4 (over z), col: 4 (over y, x), wave: 2 (over core).
Axes of the slice: x: 2, y: 2, z: 4, core: 2. Of those that a mesh axis runs over, the one named last changes fastest.
Arguments:
- transmission: float32 [4096, 4096], P('row', 'col'), may hold values from 0 to 1
- dual_focal: float32 [512, 8, 512], P(('row', 'col'), 'wave'), may hold values from -12 to 12
- dual_curvature: float32 [4096, 4096], P('row', 'col'), may hold values from -6 to 6
- pupil_mask: int32 [4096, 4096], P('row', 'col'), may hold values 0 or 1
- lyot_mask: int32 [4096, 4096], P('row', 'col'), may hold values 0 or 1
- dark_mask: int32 [512, 8, 512], P(('row', 'col'), 'wave'), may hold values 0 or 1
- focal_rows: float32 [8, 512, 4096], P('wave', None, 'row'), may hold values from -0.09375 to 0.09375
- focal_cols: float32 [8, 512, 4096], P('wave', None, 'col'), may hold values from -0.09375 to 0.09375
Outputs:
- transmission_out: float32 [4096, 4096], P('row', 'col')
- dual_focal_out: float32 [512, 8, 512], P(('row', 'col'), 'wave')
- dual_curvature_out: float32 [4096, 4096], P('row', 'col')
The draws below stay inside these ranges and needn't reach their ends.
All inputs are finite; a program needn't handle non-finite values. No bound on the sum of `pupil_mask` or of `lyot_mask` or of `dark_mask` on one device may be relied on, other than what follows from the above.
Results may differ from the reference program's by a relative error of at most 0.0001.
Values sent between devices are 32-bit elements; how exact they have to be, the bound alone decides.
A program may use at most 128 MiB of HBM per device.

```python
import jax
import jax.numpy as jnp
from jax import lax

N = 4096
Z = 512
NW = 8
ITERS = 2


def with_ends(drawn, stream_key, smallest, high):
    longest = drawn.shape.index(max(drawn.shape))
    spots = []
    for shift in (0, 1):
        where = [jax.random.randint(jax.random.fold_in(stream_key, axis), (), 0, length) for axis, length in enumerate(drawn.shape)]
        where[longest] = (where[longest] + shift) % drawn.shape[longest]
        spots.append(tuple(where))
    return drawn.at[spots[0]].set(smallest).at[spots[1]].set(high)


def steps_of(rng, extent, shards, smallest, high):
    loudness, own = 1.0, jax.random.fold_in(rng, 6)
    for dim, parts in shards:
        steps = jnp.exp(jax.random.uniform(jax.random.fold_in(own, dim), (parts,), jnp.float32, smallest / len(shards), high / len(shards)))
        loudness = loudness * jnp.repeat(steps, extent[dim] // parts).reshape([-1 if axis == dim else 1 for axis in range(len(extent))])
    return loudness


def centred(stream_key, dims, scale, most, pieces=(), held_as=jnp.bfloat16):
    drawn = jax.random.normal(stream_key, dims, jnp.float32) * scale
    if len(pieces) > 0:
        drawn = steps_of(stream_key, dims, pieces, -0.22, 0.18) * drawn
    return jnp.clip(drawn, min=-most, max=most).astype(held_as)


def setup_inputs(seed: int = 0) -> dict:
    splits = jax.random.split(jax.random.key(seed), 9)
    transmission = jnp.clip(1.0 * jax.random.uniform(splits[0], (N, N), jnp.float32) ** steps_of(splits[0], (N, N), ((0, 4), (1, 4)), -0.2, 0.2), 0.0, 1.0)
    dual_focal = centred(splits[1], (Z, NW, Z), 2.0, 12.0, ((0, 16), (1, 2)), jnp.float32)
    dual_curvature = centred(splits[2], (N, N), 1.0, 6.0, ((0, 4), (1, 4)), jnp.float32)
    pupil_mask = with_ends((jax.random.randint(splits[3], (N, N), 0, 8) < 7).astype(jnp.int32), jax.random.fold_in(splits[3], 1), 0, 1)
    lyot_mask = with_ends((jax.random.randint(splits[4], (N, N), 0, 8) < 7).astype(jnp.int32), jax.random.fold_in(splits[4], 1), 0, 1)
    dark_mask = with_ends((jax.random.randint(splits[5], (Z, NW, Z), 0, 2) < 1).astype(jnp.int32), jax.random.fold_in(splits[5], 1), 0, 1)
    focal_rows = centred(splits[6], (NW, Z, N), N ** -0.5, 0.09375, ((0, 2), (2, 4)), jnp.float32)
    focal_cols = centred(splits[7], (NW, Z, N), N ** -0.5, 0.09375, ((0, 2), (2, 4)), jnp.float32)
    return {"transmission": transmission, "dual_focal": dual_focal, "dual_curvature": dual_curvature, "pupil_mask": pupil_mask, "lyot_mask": lyot_mask, "dark_mask": dark_mask, "focal_rows": focal_rows, "focal_cols": focal_cols}


step_primal = 0.12
step_dual = 0.2
contrast = 0.5
curvature_limit = 0.1


def curvature(field):
    padded = jnp.pad(field, 1)
    beside_all = padded[2:, 1:-1] + padded[:-2, 1:-1] + padded[1:-1, 2:] + padded[1:-1, :-2]
    return 0.25 * beside_all - field


def reference(transmission, dual_focal, dual_curvature, pupil_mask, lyot_mask, dark_mask, focal_rows, focal_cols):
    highest = lax.Precision.HIGHEST
    pupil = pupil_mask.astype(jnp.float32)
    stop = pupil * lyot_mask.astype(jnp.float32)
    dark = dark_mask.astype(jnp.float32)
    primal = transmission
    dual_f = dual_focal * dark
    dual_c = dual_curvature

    def back_one(carry, items):
        rows_table, cols_table, field = items
        carried = jnp.dot(field, cols_table, precision=highest, preferred_element_type=jnp.float32)
        return carry + jnp.dot(rows_table.T, carried, precision=highest, preferred_element_type=jnp.float32), None

    def forward_one(carry, items):
        rows_table, cols_table = items
        left = jnp.dot(rows_table, carry, precision=highest, preferred_element_type=jnp.float32)
        return carry, jnp.dot(left, cols_table.T, precision=highest, preferred_element_type=jnp.float32)

    for iteration in range(ITERS):
        start = jnp.zeros((N, N), jnp.float32)
        backward, _ = lax.scan(back_one, start, (focal_rows, focal_cols, jnp.transpose(dual_f, (1, 0, 2))))
        gradient = -pupil + stop * backward + curvature(dual_c)
        primal_new = jnp.clip(primal - step_primal * gradient, 0.0, 1.0)
        extended = 2.0 * primal_new - primal
        _, fields = lax.scan(forward_one, stop * extended, (focal_rows, focal_cols))
        shifted = dual_f + step_dual * jnp.transpose(fields, (1, 0, 2))
        dual_f = dark * (shifted - step_dual * jnp.clip(shifted / step_dual, -contrast, contrast))
        moved = dual_c + step_dual * curvature(extended)
        dual_c = moved - step_dual * jnp.clip(moved / step_dual, -curvature_limit, curvature_limit)
        primal = primal_new
    return primal, dual_f, dual_c
```

```python
import jax
import jax.numpy as jnp
from jax import lax
from jax.experimental import pallas as pl
from jax.experimental.pallas import tpu as pltpu
from jax.sharding import PartitionSpec as P

ITERS = 2
step_primal = 0.12
step_dual = 0.2
contrast = 0.5
curvature_limit = 0.1
high = lax.Precision.HIGH
MESH = pl.DeviceIdType.MESH
f32 = jnp.float32
VMEM = pl.BlockSpec(memory_space=pltpu.VMEM)
ANY = pl.BlockSpec(memory_space=pl.ANY)
DMA = pltpu.SemaphoreType.DMA


def shape(*dims):
    return jax.ShapeDtypeStruct(dims, f32)


def prox(v, limit):
    return v - jnp.clip(v, -step_dual * limit, step_dual * limit)


def stencil(v, up, down, left, right):
    rows, cols = v.shape
    r = lax.broadcasted_iota(jnp.int32, v.shape, 0)
    c = lax.broadcasted_iota(jnp.int32, v.shape, 1)
    from_up = jnp.where(r == 0, up, pltpu.roll(v, 1, 0))
    from_down = jnp.where(r == rows - 1, down, pltpu.roll(v, rows - 1, 0))
    from_left = jnp.where(c == 0, left, pltpu.roll(v, 1, 1))
    from_right = jnp.where(c == cols - 1, right, pltpu.roll(v, cols - 1, 1))
    return 0.25 * (from_down + from_up + from_right + from_left) - v


def column(row):
    n = row.shape[1]
    return jnp.transpose(jnp.broadcast_to(row, (128, n)))[:, 0:1]


class Place:
    def __init__(self):
        self.r, self.c = lax.axis_index("row"), lax.axis_index("col")
        self.nr, self.nc = lax.axis_size("row"), lax.axis_size("col")
        self.na = 2 if self.nc % 2 == 0 else 1
        self.nb = self.nc // self.na
        self.a, self.b = self.c // self.nb, lax.rem(self.c, self.nb)

    def row(self, d):
        return lax.rem(self.r + d, self.nr)

    def col(self, f, e):
        return lax.rem(self.a + f, self.na) * self.nb + lax.rem(self.b + e, self.nb)

    def greet(self):
        barrier = pltpu.get_barrier_semaphore()
        for d in range(1, self.nr):
            pl.semaphore_signal(barrier, inc=1, device_id={"row": self.row(d)}, device_id_type=MESH)
        for e in range(1, self.nc):
            pl.semaphore_signal(barrier, inc=1, device_id={"col": lax.rem(self.c + e, self.nc)}, device_id_type=MESH)
        pl.semaphore_wait(barrier, self.nr + self.nc - 2)


def send(src, dst, sems, index, where):
    copy = pltpu.make_async_remote_copy(
        src_ref=src, dst_ref=dst, send_sem=sems.at[(0,) + index], recv_sem=sems.at[(1,) + index],
        device_id=where, device_id_type=MESH)
    copy.start()
    return copy


class Gather:
    def __init__(self, p, full, sems):
        self.p, self.full = p, full
        self.zs, self.bs, self.as_, self.h0, self.h1 = sems
        self.copies = {}

    @staticmethod
    def scratch(waves, nr, na, nb):
        return [DMA((2, waves, nr)), DMA((2, waves, nb)), DMA((2, waves, na)), DMA((2, waves, na, nb)), DMA((2, waves, na, nb))]

    def start(self, w):
        p = self.p
        own = self.full.at[w, p.r, p.c]
        self.copies[w] = [[send(own, own, self.zs, (w, d), {"row": p.row(d)}) for d in range(1, p.nr)], [], []]

    def forward(self, w):
        p = self.p
        for copy in self.copies[w][0]:
            copy.wait_recv()
        stack = self.full.at[w, :, p.c]
        out = self.copies[w][1]
        for e in range(1, p.nb):
            out.append(send(stack, stack, self.bs, (w, e), {"col": p.col(0, e)}))
        for f in range(1, p.na):
            out.append(send(stack, stack, self.as_, (w, f), {"col": p.col(f, 0)}))

    def relay(self, w):
        p = self.p
        half = self.full.shape[-1] // 2
        for copy in self.copies[w][1]:
            copy.wait_recv()
        out = self.copies[w][2]
        for e in range(1, p.nb):
            for f in range(1, p.na):
                low = self.full.at[w, :, p.col(0, p.nb - e), :, pl.ds(0, half)]
                out.append(send(low, low, self.h0, (w, f, e), {"col": p.col(f, 0)}))
                top = self.full.at[w, :, p.col(p.na - f, 0), :, pl.ds(half, half)]
                out.append(send(top, top, self.h1, (w, f, e), {"col": p.col(0, e)}))

    def arrive(self, w):
        for copy in self.copies[w][2]:
            copy.wait_recv()

    def finish(self):
        for groups in self.copies.values():
            for group in groups:
                for copy in group:
                    copy.wait_send()


class Scatter:
    def __init__(self, p, part, scratch):
        self.p, self.part = p, part
        self.g0, self.g1, self.gb, self.ga, self.q, self.gz = scratch[:6]
        self.s0, self.s1, self.db, self.da, self.rb, self.ra, self.zs = scratch[6:]
        self.half = part.shape[-1] // 2
        self.first, self.direct, self.second, self.third = {}, {}, {}, {}

    @staticmethod
    def scratch(waves, nr, na, nb, k, z):
        v = lambda *dims: pltpu.VMEM(dims, f32)
        return [
            v(waves, na, nb, nr, k, z // 2), v(waves, na, nb, nr, k, z // 2),
            v(waves, nb, nr, k, z), v(waves, na, nr, k, z), v(waves, nr, k, z), v(waves, nr, k, z),
            DMA((2, waves, na, nb)), DMA((2, waves, na, nb)), DMA((2, waves, nb)), DMA((2, waves, na)),
            DMA((2, waves, nb)), DMA((2, waves, na)), DMA((2, waves, nr))]

    def lanes(self, n):
        return pl.ds(n * self.half, self.half)

    def start(self, w):
        p, out = self.p, []
        for f in range(1, p.na):
            for e in range(1, p.nb):
                diagonal = self.part.at[w, :, p.col(f, e)]
                out.append(send(diagonal.at[:, :, self.lanes(0)], self.g0.at[w, f, e], self.s0, (w, f, e), {"col": p.col(f, 0)}))
                out.append(send(diagonal.at[:, :, self.lanes(1)], self.g1.at[w, f, e], self.s1, (w, f, e), {"col": p.col(0, e)}))
        self.first[w] = out

    def straight(self, w):
        p, out = self.p, []
        n = 1 if p.na > 1 else 0
        for e in range(1, p.nb):
            out.append(send(self.part.at[w, :, p.col(0, e), :, self.lanes(1)], self.gb.at[w, e, :, :, self.lanes(1)], self.db, (w, e), {"col": p.col(0, e)}))
        for f in range(1, p.na):
            out.append(send(self.part.at[w, :, p.col(f, 0), :, self.lanes(0)], self.ga.at[w, f, :, :, self.lanes(0)], self.da, (w, f), {"col": p.col(f, 0)}))
        self.direct[w] = out

    def combine(self, w):
        p, out = self.p, []
        for copy in self.first[w]:
            copy.wait_recv()
        low, top = self.lanes(0), self.lanes(1)
        keep = 1 if p.na > 1 else 0
        for e in range(1, p.nb):
            total = self.part[w, :, p.col(0, e), :, low]
            for f in range(1, p.na):
                total = total + self.g0[w, f, e]
            self.g0[w, 0, e] = total
            out.append(send(self.g0.at[w, 0, e], self.gb.at[w, e, :, :, low], self.rb, (w, e), {"col": p.col(0, e)}))
        for f in range(1, p.na):
            total = self.part[w, :, p.col(f, 0), :, top]
            for e in range(1, p.nb):
                total = total + self.g1[w, f, e]
            self.g1[w, f, 0] = total
            out.append(send(self.g1.at[w, f, 0], self.ga.at[w, f, :, :, top], self.ra, (w, f), {"col": p.col(f, 0)}))
        self.second[w] = out

    def column(self, w):
        p, out = self.p, []
        for copy in self.direct[w] + self.second[w]:
            copy.wait_recv()
        total = self.part[w, :, p.c]
        for e in range(1, p.nb):
            total = total + self.gb[w, e]
        for f in range(1, p.na):
            total = total + self.ga[w, f]
        self.q[w] = total
        for d in range(1, p.nr):
            out.append(send(self.q.at[w, p.row(d)], self.gz.at[w, d], self.zs, (w, d), {"row": p.row(d)}))
        self.third[w] = out

    def result(self, w):
        for copy in self.third[w]:
            copy.wait_recv()
        total = self.q[w, self.p.r]
        for d in range(1, self.p.nr):
            total = total + self.gz[w, d]
        return total

    def finish(self):
        for groups in (self.first, self.direct, self.second, self.third):
            for group in groups.values():
                for copy in group:
                    copy.wait_send()


class Halo:
    def __init__(self, p, scratch):
        self.p = p
        self.packed, self.rows, self.cols, self.sems = scratch

    @staticmethod
    def scratch(rows, cols):
        v = lambda *dims: pltpu.VMEM(dims, f32)
        return [v(2, 8, rows), v(2, 8, cols), v(2, 8, rows), DMA((2, 4))]

    def start(self, v):
        p = self.p
        rows, cols = v.shape
        self.packed[0] = jnp.transpose(v[:, 0:128])[0:8]
        self.packed[1] = jnp.transpose(v[:, cols - 128:cols])[120:128]
        up, down = {"row": p.row(p.nr - 1)}, {"row": p.row(1)}
        left, right = {"col": lax.rem(p.c + p.nc - 1, p.nc)}, {"col": lax.rem(p.c + 1, p.nc)}
        self.copies = [
            send(v.at[pl.ds(rows - 8, 8)], self.rows.at[0], self.sems, (0,), down),
            send(v.at[pl.ds(0, 8)], self.rows.at[1], self.sems, (1,), up),
            send(self.packed.at[1], self.cols.at[0], self.sems, (2,), right),
            send(self.packed.at[0], self.cols.at[1], self.sems, (3,), left),
        ]

    def result(self, out_r, out_c):
        p = self.p
        for copy in self.copies:
            copy.wait_recv()
        out_r[0] = jnp.where(p.r > 0, self.rows[0], 0.0)
        out_r[1] = jnp.where(p.r < p.nr - 1, self.rows[1], 0.0)
        out_c[0] = jnp.where(p.c > 0, self.cols[0], 0.0)
        out_c[1] = jnp.where(p.c < p.nc - 1, self.cols[1], 0.0)

    def finish(self):
        for copy in self.copies:
            copy.wait_send()


def curvature_step(dual, ext, edge_r, edge_c, lo, hi):
    rows, cols = dual.shape
    block = 128

    def step(i, _):
        at = pl.multiple_of(i * block, block)
        here = pl.ds(at, block)
        above = ext[pl.ds(pl.multiple_of(jnp.maximum(at - 8, 0), 8), 8), :][7:8]
        below = ext[pl.ds(pl.multiple_of(jnp.minimum(at + block, rows - 8), 8), 8), :][0:1]
        up = jnp.where(i == 0, edge_r[0, 7:8, :], above)
        down = jnp.where(i == rows // block - 1, edge_r[1, 0:1, :], below)
        left = column(edge_c[0, 7:8, here])
        right = column(edge_c[1, 0:1, here])
        moved = dual[here, :] + step_dual * stencil(ext[here, :], up, down, left, right)
        dual[here, :] = prox(moved, curvature_limit)
        return 0

    lax.fori_loop(lo, hi, step, 0)


def gather_kernel(waves, y_ref, v_ref, full, out_r, out_c, *scratch):
    p = Place()
    halo, gather = Halo(p, scratch[:4]), Gather(p, full, scratch[4:])
    p.greet()
    for w in range(waves):
        full[w, p.r, p.c] = y_ref[w]
        gather.start(w)
    halo.start(v_ref)
    for w in range(waves):
        gather.forward(w)
        if w > 0:
            gather.relay(w - 1)
    gather.relay(waves - 1)
    halo.result(out_r, out_c)
    for w in range(waves):
        gather.arrive(w)
    gather.finish()
    halo.finish()


def gather_call(y, v):
    nr, nc = lax.axis_size("row"), lax.axis_size("col")
    na = 2 if nc % 2 == 0 else 1
    waves, k, z = y.shape
    rows, cols = v.shape
    return pl.pallas_call(
        lambda *refs: gather_kernel(waves, *refs),
        in_specs=[VMEM] * 2, out_specs=[VMEM] * 3,
        out_shape=[shape(waves, nr, nc, k, z), shape(2, 8, cols), shape(2, 8, rows)],
        scratch_shapes=Halo.scratch(rows, cols) + Gather.scratch(waves, nr, na, nc // na),
        compiler_params=pltpu.CompilerParams(collective_id=0, has_side_effects=True, vmem_limit_bytes=40 << 20),
    )(y, v)


def turn_kernel(waves, again, *refs):
    part, y_ref, dark_ref, ext_hbm, dual_hbm = refs[:5]
    outs = 5 if again else 2
    y_out, dual_out = refs[5:7]
    ext, dual, local, edge_r, edge_c = refs[5 + outs:10 + outs]
    scratch = refs[10 + outs:]
    p = Place()
    load_ext = pltpu.make_async_copy(ext_hbm, ext, local.at[0])
    load_dual = pltpu.make_async_copy(dual_hbm, dual, local.at[1])
    load_ext.start()
    load_dual.start()
    halo, scatter = Halo(p, scratch[:4]), Scatter(p, part, scratch[4:17])
    p.greet()
    for w in range(waves):
        scatter.start(w)
    for w in range(min(2, waves)):
        scatter.straight(w)
    load_ext.wait()
    halo.start(ext)
    load_dual.wait()
    for w in range(waves):
        scatter.combine(w)
        if w + 2 < waves:
            scatter.straight(w + 2)
    halo.result(edge_r, edge_c)
    halo.finish()
    blocks = ext.shape[0] // 128
    if again:
        full, out_r, out_c = refs[7:10]
        gather = Gather(p, full, scratch[17:22])
        halo2 = Halo(p, scratch[22:26])

    def update(w):
        moved = y_ref[w] + step_dual * scatter.result(w)
        new = dark_ref[w] * prox(moved, contrast)
        y_out[w] = new
        if again:
            full[w, p.r, p.c] = new
            gather.start(w)

    for w in range(waves):
        scatter.column(w)
        curvature_step(dual, ext, edge_r, edge_c, blocks * w // waves, blocks * (w + 1) // waves)
        if w > 0:
            update(w - 1)
        if again and w > 1:
            gather.forward(w - 2)
    if again:
        halo2.start(dual)
    store = pltpu.make_async_copy(dual, dual_out, local.at[2])
    store.start()
    update(waves - 1)
    if again:
        for w in range(max(0, waves - 2), waves):
            gather.forward(w)
            if w > 1:
                gather.relay(w - 2)
        for w in range(max(0, waves - 2), waves):
            gather.relay(w)
        halo2.result(out_r, out_c)
        for w in range(waves):
            gather.arrive(w)
        gather.finish()
        halo2.finish()
    scatter.finish()
    store.wait()


def turn_call(part, y, dark, ext, dual, again):
    nr, nc = lax.axis_size("row"), lax.axis_size("col")
    na = 2 if nc % 2 == 0 else 1
    nb = nc // na
    waves, k, z = y.shape
    rows, cols = ext.shape
    v = lambda *dims: pltpu.VMEM(dims, f32)
    out_shape = [shape(waves, k, z), shape(rows, cols)]
    out_specs = [VMEM, ANY]
    scratch = [v(rows, cols), v(rows, cols), DMA((3,)), v(2, 8, cols), v(2, 8, rows)]
    scratch += Halo.scratch(rows, cols) + Scatter.scratch(waves, nr, na, nb, k, z)
    if again:
        out_shape += [shape(waves, nr, nc, k, z), shape(2, 8, cols), shape(2, 8, rows)]
        out_specs += [VMEM] * 3
        scratch += Gather.scratch(waves, nr, na, nb) + Halo.scratch(rows, cols)
    return pl.pallas_call(
        lambda *refs: turn_kernel(waves, again, *refs),
        in_specs=[VMEM] * 3 + [ANY] * 2, out_specs=out_specs, out_shape=out_shape, scratch_shapes=scratch,
        compiler_params=pltpu.CompilerParams(collective_id=1 if again else 2, has_side_effects=True, vmem_limit_bytes=50 << 20),
    )(part.reshape(waves, nr, nc, k, z), y, dark, ext, dual)


def primal_kernel(mine, other, primal, pupil_m, lyot_m, dual, above, below, edge_r, edge_c, new_ref, ext_ref, mask_ref):
    i, last = pl.program_id(0), pl.num_programs(0) - 1
    pupil = pupil_m[...].astype(f32)
    stop = pupil * lyot_m[...].astype(f32)
    x = primal[...]
    up = jnp.where(i == 0, edge_r[0, 7:8, :], above[7:8, :])
    down = jnp.where(i == last, edge_r[1, 0:1, :], below[0:1, :])
    curv = stencil(dual[...], up, down, column(edge_c[0, 7:8, :]), column(edge_c[1, 0:1, :]))
    gradient = stop * (mine[...] + other[...]) - pupil + curv
    new = jnp.clip(x - step_primal * gradient, 0.0, 1.0)
    ext = 2.0 * new - x
    new_ref[...] = new
    ext_ref[...] = ext
    mask_ref[...] = stop * ext


def primal_step(mine, other, primal, pupil, lyot, dual, edge_r, edge_c):
    rows, cols = primal.shape
    block = 128
    steps, eights = rows // block, block // 8
    whole = pl.BlockSpec((block, cols), lambda i: (i, 0))
    specs = [
        pl.BlockSpec((8, cols), lambda i: (jnp.maximum(i * eights - 1, 0), 0)),
        pl.BlockSpec((8, cols), lambda i: (jnp.minimum((i + 1) * eights, steps * eights - 1), 0)),
        pl.BlockSpec((2, 8, cols), lambda i: (0, 0, 0)),
        pl.BlockSpec((2, 8, block), lambda i: (0, 0, i)),
    ]
    return pl.pallas_call(
        primal_kernel,
        grid=(steps,),
        in_specs=[whole] * 6 + specs,
        out_specs=[whole] * 3,
        out_shape=[shape(rows, cols)] * 3,
        cost_estimate=pl.CostEstimate(flops=30 * rows * cols, bytes_accessed=36 * rows * cols, transcendentals=0),
    )(mine, other, primal, pupil, lyot, dual, dual, dual, edge_r, edge_c)


def other_waves(part):
    n = lax.axis_size("wave")
    if n == 1:
        return jnp.zeros_like(part)
    if n == 2:
        return lax.ppermute(part, "wave", [(0, 1), (1, 0)])
    return lax.psum(part, "wave") - part


def per_device(transmission, dual_focal, dual_curvature, pupil_mask, lyot_mask, dark_mask, focal_rows, focal_cols):
    waves, z = dual_focal.shape[1:]
    dark = jnp.transpose(dark_mask, (1, 0, 2)).astype(f32)
    y = jnp.transpose(dual_focal, (1, 0, 2)) * dark
    primal, dual = transmission, dual_curvature
    full, edge_r, edge_c = gather_call(y, dual)
    for iteration in range(ITERS):
        full = full.reshape(waves, -1, z)
        carried = jnp.einsum("wkz,wzc->wkc", full, focal_cols, precision=high)
        backward = jnp.einsum("wkr,wkc->rc", focal_rows, carried, precision=high)
        other = other_waves(backward)
        primal, extended, masked = primal_step(backward, other, primal, pupil_mask, lyot_mask, dual, edge_r, edge_c)
        left = jnp.einsum("wkr,rc->wkc", focal_rows, masked, precision=high)
        part = jnp.einsum("wkc,wzc->wkz", left, focal_cols, precision=high)
        if iteration < ITERS - 1:
            y, dual, full, edge_r, edge_c = turn_call(part, y, dark, extended, dual, True)
        else:
            y, dual = turn_call(part, y, dark, extended, dual, False)
    return primal, jnp.transpose(y, (1, 0, 2)), dual


def solution(mesh):
    return jax.shard_map(
        per_device,
        mesh=mesh,
        in_specs=(
            P("row", "col"),
            P(("row", "col"), "wave", None),
            P("row", "col"),
            P("row", "col"),
            P("row", "col"),
            P(("row", "col"), "wave", None),
            P("wave", None, "row"),
            P("wave", None, "col"),
        ),
        out_specs=(P("row", "col"), P(("row", "col"), "wave", None), P("row", "col")),
        check_vma=False,
    )
```

```python
import types

import jax
import jax.numpy as jnp
from jax import lax
from jax.experimental import pallas as pl
from jax.experimental.pallas import tpu as pltpu
from jax.sharding import PartitionSpec as P

ITERS = 2
step_primal = 0.12
step_dual = 0.2
contrast = 0.5
curvature_limit = 0.1
BLOCK = 128
LIMIT = 61 << 20
MESH = pl.DeviceIdType.MESH
f32, bf16 = jnp.float32, jnp.bfloat16
VMEM = pl.BlockSpec(memory_space=pltpu.VMEM)
ANY = pl.BlockSpec(memory_space=pl.ANY)
DMA = pltpu.SemaphoreType.DMA


def shape(*dims, kind=f32):
    return jax.ShapeDtypeStruct(dims, kind)


def prox(v, limit):
    return v - jnp.clip(v, -step_dual * limit, step_dual * limit)


def stencil(v, up, down, left, right):
    rows, cols = v.shape
    r = lax.broadcasted_iota(jnp.int32, v.shape, 0)
    c = lax.broadcasted_iota(jnp.int32, v.shape, 1)
    from_up = jnp.where(r == 0, up, pltpu.roll(v, 1, 0))
    from_down = jnp.where(r == rows - 1, down, pltpu.roll(v, rows - 1, 0))
    from_left = jnp.where(c == 0, left, pltpu.roll(v, 1, 1))
    from_right = jnp.where(c == cols - 1, right, pltpu.roll(v, cols - 1, 1))
    return 0.25 * (from_down + from_up + from_right + from_left) - v


def column(row):
    n = row.shape[1]
    return jnp.transpose(jnp.broadcast_to(row, (128, n)))[:, 0:1]


class Place:
    def __init__(self):
        self.r, self.c = lax.axis_index("row"), lax.axis_index("col")
        self.nr, self.nc = lax.axis_size("row"), lax.axis_size("col")
        self.na = 2 if self.nc % 2 == 0 else 1
        self.nb = self.nc // self.na
        self.w, self.nw = lax.axis_index("wave"), lax.axis_size("wave")
        self.a, self.b = self.c // self.nb, lax.rem(self.c, self.nb)

    def wave(self, n):
        return {"wave": lax.rem(self.w + n, self.nw)}

    def row(self, d):
        return lax.rem(self.r + d, self.nr)

    def col(self, f, e):
        return lax.rem(self.a + f, self.na) * self.nb + lax.rem(self.b + e, self.nb)

    def greet(self, waves):
        barrier = pltpu.get_barrier_semaphore()
        for d in range(1, self.nr):
            pl.semaphore_signal(barrier, inc=1, device_id={"row": self.row(d)}, device_id_type=MESH)
        for e in range(1, self.nc):
            pl.semaphore_signal(barrier, inc=1, device_id={"col": lax.rem(self.c + e, self.nc)}, device_id_type=MESH)
        peers = self.nr + self.nc - 2
        if waves:
            for n in range(1, self.nw):
                pl.semaphore_signal(barrier, inc=1, device_id=self.wave(n), device_id_type=MESH)
            peers += self.nw - 1
        pl.semaphore_wait(barrier, peers)


def send(src, dst, sems, index, where):
    copy = pltpu.make_async_remote_copy(
        src_ref=src, dst_ref=dst, send_sem=sems.at[(0,) + index], recv_sem=sems.at[(1,) + index],
        device_id=where, device_id_type=MESH)
    copy.start()
    return copy


class Gather:
    def __init__(self, p, full, sems):
        self.p, self.full = p, full
        self.zs, self.bs, self.as_, self.h0, self.h1 = sems
        self.along, self.across, self.relays = {}, {}, {}

    @staticmethod
    def scratch(waves, nr, na, nb):
        return [DMA((2, waves, nr)), DMA((2, waves, nr, nb)), DMA((2, waves, nr, na)), DMA((2, waves, na, nb)), DMA((2, waves, na, nb))]

    def spread(self, w, d):
        p = self.p
        block = self.full.at[w, p.row(p.nr - d) if d else p.r, p.c]
        out = self.across.setdefault(w, [])
        for e in range(1, p.nb):
            out.append(send(block, block, self.bs, (w, d, e), {"col": p.col(0, e)}))
        for f in range(1, p.na):
            out.append(send(block, block, self.as_, (w, d, f), {"col": p.col(f, 0)}))

    def start(self, w):
        p = self.p
        own = self.full.at[w, p.r, p.c]
        self.along[w] = [send(own, own, self.zs, (w, d), {"row": p.row(d)}) for d in range(1, p.nr)]

    def forward(self, w):
        for d in range(1, self.p.nr):
            self.along[w][d - 1].wait_recv()
            self.spread(w, d)

    def relay(self, w):
        p = self.p
        half = self.full.shape[-1] // 2
        for copy in self.across[w]:
            copy.wait_recv()
        out = self.relays[w] = []
        for e in range(1, p.nb):
            for f in range(1, p.na):
                low = self.full.at[w, :, p.col(0, p.nb - e), :, pl.ds(0, half)]
                out.append(send(low, low, self.h0, (w, f, e), {"col": p.col(f, 0)}))
                top = self.full.at[w, :, p.col(p.na - f, 0), :, pl.ds(half, half)]
                out.append(send(top, top, self.h1, (w, f, e), {"col": p.col(0, e)}))

    def arrive(self, w):
        for copy in self.relays[w]:
            copy.wait_recv()

    def finish(self):
        for groups in (self.along, self.across, self.relays):
            for group in groups.values():
                for copy in group:
                    copy.wait_send()


class Scatter:
    def __init__(self, p, part, scratch):
        self.p, self.part = p, part
        self.g0, self.g1, self.gb, self.ga, self.q, self.gz = scratch[:6]
        self.s0, self.s1, self.db, self.da, self.rb, self.ra, self.zs = scratch[6:]
        self.half = part.shape[-1] // 2
        self.first, self.direct, self.second, self.third = {}, {}, {}, {}

    @staticmethod
    def scratch(waves, nr, na, nb, k, z):
        v = lambda *dims: pltpu.VMEM(dims, f32)
        fa, fb = max(na - 1, 1), max(nb - 1, 1)
        return [
            v(waves, fa, fb, nr, k, z // 2), v(waves, fa, fb, nr, k, z // 2),
            v(waves, fb, nr, k, z), v(waves, fa, nr, k, z), v(waves, nr, k, z), v(waves, nr, k, z),
            DMA((2, waves, na, nb)), DMA((2, waves, na, nb)), DMA((2, waves, nb)), DMA((2, waves, na)),
            DMA((2, waves, nb)), DMA((2, waves, na)), DMA((2, waves, nr))]

    def lanes(self, n):
        return pl.ds(n * self.half, self.half)

    def start(self, w):
        p, out = self.p, []
        for f in range(1, p.na):
            for e in range(1, p.nb):
                diagonal = self.part.at[w, :, p.col(f, e)]
                out.append(send(diagonal.at[:, :, self.lanes(0)], self.g0.at[w, f - 1, e - 1], self.s0, (w, f, e), {"col": p.col(f, 0)}))
                out.append(send(diagonal.at[:, :, self.lanes(1)], self.g1.at[w, f - 1, e - 1], self.s1, (w, f, e), {"col": p.col(0, e)}))
        self.first[w] = out

    def straight(self, w):
        p, out = self.p, []
        low, top = self.lanes(0), self.lanes(1)
        for e in range(1, p.nb):
            out.append(send(self.part.at[w, :, p.col(0, e), :, top], self.gb.at[w, e - 1, :, :, top], self.db, (w, e), {"col": p.col(0, e)}))
        for f in range(1, p.na):
            out.append(send(self.part.at[w, :, p.col(f, 0), :, low], self.ga.at[w, f - 1, :, :, low], self.da, (w, f), {"col": p.col(f, 0)}))
        self.direct[w] = out

    def combine(self, w):
        p, out = self.p, []
        for copy in self.first[w]:
            copy.wait_recv()
        low, top = self.lanes(0), self.lanes(1)
        for e in range(1, p.nb):
            total = self.part[w, :, p.col(0, e), :, low]
            for f in range(1, p.na):
                total = total + self.g0[w, f - 1, e - 1]
            self.g0[w, 0, e - 1] = total
            out.append(send(self.g0.at[w, 0, e - 1], self.gb.at[w, e - 1, :, :, low], self.rb, (w, e), {"col": p.col(0, e)}))
        for f in range(1, p.na):
            total = self.part[w, :, p.col(f, 0), :, top]
            for e in range(1, p.nb):
                total = total + self.g1[w, f - 1, e - 1]
            self.g1[w, f - 1, 0] = total
            out.append(send(self.g1.at[w, f - 1, 0], self.ga.at[w, f - 1, :, :, top], self.ra, (w, f), {"col": p.col(f, 0)}))
        self.second[w] = out

    def column(self, w):
        p, out = self.p, []
        for copy in self.direct[w] + self.second[w]:
            copy.wait_recv()
        total = self.part[w, :, p.c]
        for e in range(1, p.nb):
            total = total + self.gb[w, e - 1]
        for f in range(1, p.na):
            total = total + self.ga[w, f - 1]
        self.q[w] = total
        for d in range(1, p.nr):
            out.append(send(self.q.at[w, p.row(d)], self.gz.at[w, d], self.zs, (w, d), {"row": p.row(d)}))
        self.third[w] = out

    def result(self, w):
        for copy in self.third[w]:
            copy.wait_recv()
        total = self.q[w, self.p.r]
        for d in range(1, self.p.nr):
            total = total + self.gz[w, d]
        return total

    def finish(self):
        for groups in (self.first, self.direct, self.second, self.third):
            for group in groups.values():
                for copy in group:
                    copy.wait_send()

class Halo:
    def __init__(self, p, scratch):
        self.p = p
        self.packed, self.rows, self.cols, self.sems = scratch

    @staticmethod
    def scratch(rows, cols):
        v = lambda *dims: pltpu.VMEM(dims, f32)
        return [v(2, 8, rows), v(2, 8, cols), v(2, 8, rows), DMA((2, 4))]

    def start(self, v):
        p = self.p
        rows, cols = v.shape
        self.packed[0] = jnp.transpose(v[:, 0:128])[0:8]
        self.packed[1] = jnp.transpose(v[:, cols - 128:cols])[120:128]
        up, down = {"row": p.row(p.nr - 1)}, {"row": p.row(1)}
        left, right = {"col": lax.rem(p.c + p.nc - 1, p.nc)}, {"col": lax.rem(p.c + 1, p.nc)}
        self.copies = [
            send(v.at[pl.ds(rows - 8, 8)], self.rows.at[0], self.sems, (0,), down),
            send(v.at[pl.ds(0, 8)], self.rows.at[1], self.sems, (1,), up),
            send(self.packed.at[1], self.cols.at[0], self.sems, (2,), right),
            send(self.packed.at[0], self.cols.at[1], self.sems, (3,), left),
        ]

    def result(self, out_r, out_c):
        p = self.p
        for copy in self.copies:
            copy.wait_recv()
        out_r[0] = jnp.where(p.r > 0, self.rows[0], 0.0)
        out_r[1] = jnp.where(p.r < p.nr - 1, self.rows[1], 0.0)
        out_c[0] = jnp.where(p.c > 0, self.cols[0], 0.0)
        out_c[1] = jnp.where(p.c < p.nc - 1, self.cols[1], 0.0)

    def finish(self):
        for copy in self.copies:
            copy.wait_send()


def curvature(v, i, block, edge_r, edge_c):
    rows = v.shape[0]
    at = pl.multiple_of(i * block, block)
    here = pl.ds(at, block)
    above = v[pl.ds(pl.multiple_of(jnp.maximum(at - 8, 0), 8), 8), :][7:8]
    below = v[pl.ds(pl.multiple_of(jnp.minimum(at + block, rows - 8), 8), 8), :][0:1]
    up = jnp.where(i == 0, edge_r[0, 7:8, :], above)
    down = jnp.where(i == rows // block - 1, edge_r[1, 0:1, :], below)
    return stencil(v[here, :], up, down, column(edge_c[0, 7:8, here]), column(edge_c[1, 0:1, here]))


def curvature_step(dual, ext, edge_r, edge_c, lo, hi):
    def step(i, _):
        here = pl.ds(pl.multiple_of(i * BLOCK, BLOCK), BLOCK)
        moved = dual[here, :] + step_dual * curvature(ext, i, BLOCK, edge_r, edge_c)
        dual[here, :] = prox(moved, curvature_limit)
        return 0

    lax.fori_loop(lo, hi, step, 0)


def split(v):
    top = v.astype(bf16)
    return top, (v - top.astype(f32)).astype(bf16)


def dot3(a, b, over):
    def dot(u, v):
        return lax.dot_general(u, v, (over, ((), ())), preferred_element_type=f32)

    return dot(a[0], b[0]) + dot(a[0], b[1]) + dot(a[1], b[0])


def forward_chunk(m, w):
    u, cols = m.lh.shape
    step = min(512, cols)
    for n in range(cols // step):
        j = pl.ds(n * step, step)
        m.lh[:, j], m.ll[:, j] = split(dot3((m.rh[w], m.rl[w]), (m.ah[:, j], m.al[:, j]), ((1,), (0,))))
    out = dot3((m.lh[...], m.ll[...]), (m.ch[w], m.cl[w]), ((1,), (1,)))
    m.part[w] = out.reshape(m.part.shape[1:])


def back_tile(m, w, t, size):
    rows, cols = m.acc.shape
    i = pl.ds(pl.multiple_of(t * size, size), size)
    s = split(dot3((m.rh[w, :, i], m.rl[w, :, i]), (m.yh[...], m.yl[...]), ((0,), (0,))))
    m.sh[...], m.sl[...] = s
    step = min(512, cols)
    for n in range(cols // step):
        j = pl.ds(n * step, step)
        new = dot3((m.sh[...], m.sl[...]), (m.ch[w, :, j], m.cl[w, :, j]), ((1,), (0,)))
        m.acc[i, j] = new if w == 0 else m.acc[i, j] + new


class Primal:
    def __init__(self, p, m):
        self.p, self.m = p, m
        rows = m.acc.shape[0]
        self.size = m.sh.shape[0]
        self.tiles = rows // self.size
        self.sent = []

    @staticmethod
    def scratch(rows, cols, nw, tile):
        v = lambda *dims: pltpu.VMEM(dims, f32)
        i32 = lambda *dims: pltpu.VMEM(dims, jnp.int32)
        return dict(
            acc=v(rows, cols), other=v(max(nw - 1, 1), rows, cols), wave_sems=DMA((2, rows // tile, nw)),
            x_in=v(2, BLOCK, cols), pupil_in=i32(2, BLOCK, cols), lyot_in=i32(2, BLOCK, cols), in_sems=DMA((2, 3)),
            out_sems=DMA((rows // tile, 4)))

    def load(self, i, slot):
        m = self.m
        here = pl.ds(pl.multiple_of(i * BLOCK, BLOCK), BLOCK)
        pairs = ((m.x, m.x_in), (m.pupil, m.pupil_in), (m.lyot, m.lyot_in))
        return [pltpu.make_async_copy(a.at[here], b.at[slot], m.in_sems.at[slot, n]) for n, (a, b) in enumerate(pairs)]

    def begin(self):
        for i in range(2):
            for copy in self.load(i, i):
                copy.start()

    def exchange(self, t):
        p, m = self.p, self.m
        here = pl.ds(t * self.size, self.size)
        self.sent.append([send(m.acc.at[here], m.other.at[n - 1, here], m.wave_sems, (t, n), p.wave(n)) for n in range(1, p.nw)])

    def step(self, i):
        p, m = self.p, self.m
        slot = lax.rem(i, 2)
        here = pl.ds(pl.multiple_of(i * BLOCK, BLOCK), BLOCK)
        for copy in self.load(i, slot):
            copy.wait()
        pupil = m.pupil_in[slot].astype(f32)
        stop = pupil * m.lyot_in[slot].astype(f32)
        x = m.x_in[slot]
        total = m.acc[here, :]
        for n in range(1, p.nw):
            total = total + m.other[n - 1, here, :]
        gradient = stop * total - pupil + curvature(m.dual_v, i, BLOCK, m.dual_r, m.dual_c)
        new = jnp.clip(x - step_primal * gradient, 0.0, 1.0)
        ext = 2.0 * new - x
        m.acc[here, :] = new
        m.ext_v[here, :] = ext
        m.ah[here, :], m.al[here, :] = split(stop * ext)

        @pl.when(i + 2 < m.acc.shape[0] // BLOCK)
        def _():
            for copy in self.load(i + 2, slot):
                copy.start()

        return 0

    def finish(self):
        m, out = self.m, []
        for t in range(self.tiles):
            for copy in self.sent[t]:
                copy.wait()
            per = self.size // BLOCK
            lax.fori_loop(t * per, (t + 1) * per, lambda i, _: self.step(i), 0)
            here = pl.ds(t * self.size, self.size)
            pairs = ((m.acc, m.x_out), (m.ext_v, m.ext_out), (m.ah, m.ah_out), (m.al, m.al_out))
            for n, (a, b) in enumerate(pairs):
                out.append(pltpu.make_async_copy(a.at[here], b.at[here], m.out_sems.at[t, n]))
                out[-1].start()
        for copy in out:
            copy.wait()


def back_chunk(m, w, gather, primal):
    gather.arrive(w)
    y = m.full[w].reshape(m.yh.shape)
    m.yh[...], m.yl[...] = split(y)
    if w < m.full.shape[0] - 1:
        lax.fori_loop(0, primal.tiles, lambda t, _: (back_tile(m, w, t, primal.size), 0)[1], 0)
    else:
        for t in range(primal.tiles):
            back_tile(m, w, t, primal.size)
            primal.exchange(t)


def first_kernel(m):
    waves = m.full.shape[0]
    p = Place()
    halo, gather, primal = Halo(p, m.halo), Gather(p, m.full, m.gather), Primal(p, m)
    load_dual = pltpu.make_async_copy(m.dual, m.dual_v, m.local.at[0])
    load_dual.start()

    def stage(w):
        return [pltpu.make_async_copy(a.at[w], b.at[w % 2], m.stage_sems.at[w % 2, n])
                for n, (a, b) in enumerate(((m.rows, m.rows_in), (m.cols, m.cols_in)))]

    for w in range(min(2, waves)):
        for copy in stage(w):
            copy.start()
    primal.begin()
    p.greet(True)
    for w in range(waves):
        m.full[w, p.r, p.c] = m.y[w]
    for w in range(waves):
        if w < 2:
            gather.start(w)
        gather.spread(w, 0)
    load_dual.wait()
    halo.start(m.dual_v)
    saves = []
    for w in range(waves):
        for copy in stage(w):
            copy.wait()
        m.rh[w], m.rl[w] = split(m.rows_in[w % 2])
        m.ch[w], m.cl[w] = split(m.cols_in[w % 2])
        if w + 2 < waves:
            for copy in stage(w + 2):
                copy.start()
        for n, (a, b) in enumerate(((m.rh, m.rh_out), (m.rl, m.rl_out), (m.ch, m.ch_out), (m.cl, m.cl_out))):
            saves.append(pltpu.make_async_copy(a.at[w], b.at[w], m.save_sems.at[w, n]))
            saves[-1].start()
        gather.forward(w)
        if w + 2 < waves:
            gather.start(w + 2)
        if w > 0:
            gather.relay(w - 1)
    halo.result(m.dual_r, m.dual_c)
    for w in range(waves):
        if w == 0:
            gather.relay(waves - 1)
        back_chunk(m, w, gather, primal)
    gather.finish()
    halo.finish()
    primal.finish()
    for copy in saves:
        copy.wait()


def turn_kernel(m, again):
    waves = m.part.shape[0]
    p = Place()
    loads = {w: [pltpu.make_async_copy(a.at[w], b.at[w], m.load_sems.at[w, n])
                 for n, (a, b) in enumerate(((m.rh_in, m.rh), (m.rl_in, m.rl), (m.ch_in, m.ch), (m.cl_in, m.cl)))]
             for w in range(waves)}
    pairs = ((m.ah_in, m.ah), (m.al_in, m.al), (m.ext, m.ext_v), (m.dual, m.dual_v))
    local = [pltpu.make_async_copy(a, b, m.local.at[n]) for n, (a, b) in enumerate(pairs)]
    local[0].start()
    local[1].start()
    for w in range(waves):
        for copy in loads[w]:
            copy.start()
        if w == 0:
            local[2].start()
            local[3].start()
    halo, scatter = Halo(p, m.halo), Scatter(p, m.part, m.scatter)
    if again:
        gather, primal, halo2 = Gather(p, m.full, m.gather), Primal(p, m), Halo(p, m.halo2)
    p.greet(again)
    local[0].wait()
    local[1].wait()
    store = pltpu.make_async_copy(m.dual_v, m.dual_out, m.local.at[4])
    blocks = m.ext_v.shape[0] // BLOCK
    for t in range(2 * waves + 4):
        if t < waves:
            for copy in loads[t]:
                copy.wait()
            forward_chunk(m, t)
            scatter.start(t)
        elif t < 2 * waves:
            w = t - waves
            if w == 0:
                halo.result(m.ext_r, m.ext_c)
                halo.finish()
                local[3].wait()
            curvature_step(m.dual_v, m.ext_v, m.ext_r, m.ext_c, blocks * w // waves, blocks * (w + 1) // waves)
            if w == waves - 1:
                store.start()
                if again:
                    halo2.start(m.dual_v)
                    primal.begin()
        if t == 0:
            local[2].wait()
            halo.start(m.ext_v)
        if 0 <= t - 1 < waves:
            scatter.combine(t - 1)
            scatter.straight(t - 1)
        if 0 <= t - 2 < waves:
            scatter.column(t - 2)
        if 0 <= t - 3 < waves:
            w = t - 3
            moved = m.y[w] + step_dual * scatter.result(w)
            new = m.dark[w] * prox(moved, contrast)
            m.y_out[w] = new
            if again:
                m.full[w, p.r, p.c] = new
                gather.start(w)
                gather.spread(w, 0)
        if again:
            if 0 <= t - 4 < waves:
                gather.forward(t - 4)
            if 0 <= t - 5 < waves:
                gather.relay(t - 5)
    scatter.finish()
    if again:
        for w in range(waves):
            if w == waves - 1:
                halo2.result(m.dual_r, m.dual_c)
                halo2.finish()
            back_chunk(m, w, gather, primal)
        gather.finish()
        primal.finish()
    store.wait()


def call(kernel, ins, outs, scratch, collective_id):
    names, flat, counts = list(ins) + list(outs), [], {}
    for name, what in scratch.items():
        counts[name] = len(what) if isinstance(what, list) else None
        flat += what if isinstance(what, list) else [what]

    def body(*refs):
        m = types.SimpleNamespace(**dict(zip(names, refs)))
        rest = list(refs[len(names):])
        for name, count in counts.items():
            setattr(m, name, [rest.pop(0) for _ in range(count)] if count is not None else rest.pop(0))
        kernel(m)

    out = pl.pallas_call(
        body,
        in_specs=[spec for _, spec in ins.values()], out_specs=[spec for _, spec in outs.values()],
        out_shape=[what for what, _ in outs.values()], scratch_shapes=flat,
        compiler_params=pltpu.CompilerParams(collective_id=collective_id, has_side_effects=True, vmem_limit_bytes=LIMIT),
    )(*[value for value, _ in ins.values()])
    return types.SimpleNamespace(**dict(zip(outs, out)))


def sizes():
    nr, nc, nw = lax.axis_size("row"), lax.axis_size("col"), lax.axis_size("wave")
    na = 2 if nc % 2 == 0 else 1
    return nr, nc, nw, na, nc // na


def common(waves, u, z, rows, cols):
    nr, nc, nw, na, nb = sizes()
    tile = min(512, rows)
    b = lambda *dims: pltpu.VMEM(dims, bf16)
    v = lambda *dims: pltpu.VMEM(dims, f32)
    held = dict(rh=b(waves, u, rows), rl=b(waves, u, rows), ch=b(waves, z, cols), cl=b(waves, z, cols),
                ah=b(rows, cols), al=b(rows, cols), ext_v=v(rows, cols), dual_v=v(rows, cols), local=DMA((5,)), halo=Halo.scratch(rows, cols))
    back = dict(sh=b(tile, z), sl=b(tile, z), yh=b(u, z), yl=b(u, z), dual_r=v(2, 8, cols), dual_c=v(2, 8, rows),
                gather=Gather.scratch(waves, nr, na, nb), **Primal.scratch(rows, cols, nw, tile))
    outs = dict(x_out=(shape(rows, cols), ANY), ext_out=(shape(rows, cols), ANY), ah_out=(shape(rows, cols, kind=bf16), ANY),
                al_out=(shape(rows, cols, kind=bf16), ANY))
    return held, back, outs


def first(y, x, dual, pupil, lyot, focal_rows, focal_cols):
    nr, nc, nw, na, nb = sizes()
    waves, k, z = y.shape
    u = focal_rows.shape[1]
    rows, cols = x.shape
    held, back, outs = common(waves, u, z, rows, cols)
    for name, like in (("rh_out", focal_rows), ("rl_out", focal_rows), ("ch_out", focal_cols), ("cl_out", focal_cols)):
        outs[name] = (shape(*like.shape, kind=bf16), ANY)
    scratch = dict(full=pltpu.VMEM((waves, nr, nc, k, z), f32), rows_in=pltpu.VMEM((2, u, rows), f32), cols_in=pltpu.VMEM((2, z, cols), f32),
                   stage_sems=DMA((2, 2)), save_sems=DMA((waves, 4)), **held, **back)
    ins = dict(y=(y, VMEM), x=(x, ANY), dual=(dual, ANY), pupil=(pupil, ANY), lyot=(lyot, ANY), rows=(focal_rows, ANY), cols=(focal_cols, ANY))
    return call(first_kernel, ins, outs, scratch, 0)


def turn(f, h, y, dark, dual, pupil, lyot, again):
    nr, nc, nw, na, nb = sizes()
    waves, k, z = y.shape
    u = f.rh_out.shape[1]
    rows, cols = dual.shape
    v = lambda *dims: pltpu.VMEM(dims, f32)
    held, back, outs = common(waves, u, z, rows, cols)
    scratch = dict(part=v(waves, nr, nc, k, z), lh=pltpu.VMEM((u, cols), bf16), ll=pltpu.VMEM((u, cols), bf16), load_sems=DMA((waves, 4)),
                   ext_r=v(2, 8, cols), ext_c=v(2, 8, rows), scatter=Scatter.scratch(waves, nr, na, nb, k, z), **held)
    ins = dict(y=(y, VMEM), dark=(dark, VMEM), ext=(h.ext_out, ANY), dual=(dual, ANY), ah_in=(h.ah_out, ANY), al_in=(h.al_out, ANY),
               rh_in=(f.rh_out, ANY), rl_in=(f.rl_out, ANY), ch_in=(f.ch_out, ANY), cl_in=(f.cl_out, ANY))
    ends = dict(y_out=(shape(waves, k, z), VMEM), dual_out=(shape(rows, cols), ANY))
    if again:
        ins.update(x=(h.x_out, ANY), pupil=(pupil, ANY), lyot=(lyot, ANY))
        scratch.update(full=v(waves, nr, nc, k, z), halo2=Halo.scratch(rows, cols), **back)
        ends.update(outs)
    return call(lambda m: turn_kernel(m, again), ins, ends, scratch, 1 if again else 2)


def per_device(transmission, dual_focal, dual_curvature, pupil_mask, lyot_mask, dark_mask, focal_rows, focal_cols):
    dark = jnp.transpose(dark_mask, (1, 0, 2)).astype(f32)
    y = jnp.transpose(dual_focal, (1, 0, 2)) * dark
    dual = dual_curvature
    f = h = first(y, transmission, dual, pupil_mask, lyot_mask, focal_rows, focal_cols)
    for iteration in range(ITERS):
        x = h.x_out
        h = turn(f, h, y, dark, dual, pupil_mask, lyot_mask, iteration < ITERS - 1)
        y, dual = h.y_out, h.dual_out
    return x, jnp.transpose(y, (1, 0, 2)), dual


def solution(mesh):
    return jax.shard_map(
        per_device,
        mesh=mesh,
        in_specs=(
            P("row", "col"),
            P(("row", "col"), "wave", None),
            P("row", "col"),
            P("row", "col"),
            P("row", "col"),
            P(("row", "col"), "wave", None),
            P("wave", None, "row"),
            P("wave", None, "col"),
        ),
        out_specs=(P("row", "col"), P(("row", "col"), "wave", None), P("row", "col")),
        check_vma=False,
    )
```

```python
import types

import jax
import jax.numpy as jnp
from jax import lax
from jax.experimental import pallas as pl
from jax.experimental.pallas import tpu as pltpu
from jax.sharding import PartitionSpec as P

ITERS = 2
step_primal = 0.12
step_dual = 0.2
contrast = 0.5
curvature_limit = 0.1
BLOCK = 128
LIMIT = 61 << 20
MESH = pl.DeviceIdType.MESH
f32, bf16 = jnp.float32, jnp.bfloat16
VMEM = pl.BlockSpec(memory_space=pltpu.VMEM)
ANY = pl.BlockSpec(memory_space=pl.ANY)
DMA = pltpu.SemaphoreType.DMA


def shape(*dims, kind=f32):
    return jax.ShapeDtypeStruct(dims, kind)


def prox(v, limit):
    return v - jnp.clip(v, -step_dual * limit, step_dual * limit)


def stencil(v, up, down, left, right):
    rows, cols = v.shape
    r = lax.broadcasted_iota(jnp.int32, v.shape, 0)
    c = lax.broadcasted_iota(jnp.int32, v.shape, 1)
    from_up = jnp.where(r == 0, up, pltpu.roll(v, 1, 0))
    from_down = jnp.where(r == rows - 1, down, pltpu.roll(v, rows - 1, 0))
    from_left = jnp.where(c == 0, left, pltpu.roll(v, 1, 1))
    from_right = jnp.where(c == cols - 1, right, pltpu.roll(v, cols - 1, 1))
    return 0.25 * (from_down + from_up + from_right + from_left) - v


def column(row):
    n = row.shape[1]
    return jnp.transpose(jnp.broadcast_to(row, (128, n)))[:, 0:1]


class Place:
    def __init__(self):
        self.r, self.c = lax.axis_index("row"), lax.axis_index("col")
        self.nr, self.nc = lax.axis_size("row"), lax.axis_size("col")
        self.na = 2 if self.nc % 2 == 0 else 1
        self.nb = self.nc // self.na
        self.w, self.nw = lax.axis_index("wave"), lax.axis_size("wave")
        self.a, self.b = self.c // self.nb, lax.rem(self.c, self.nb)

    def wave(self, n):
        return {"wave": lax.rem(self.w + n, self.nw)}

    def row(self, d):
        return lax.rem(self.r + d, self.nr)

    def col(self, f, e):
        return lax.rem(self.a + f, self.na) * self.nb + lax.rem(self.b + e, self.nb)

    def greet(self, waves):
        barrier = pltpu.get_barrier_semaphore()
        for d in range(1, self.nr):
            pl.semaphore_signal(barrier, inc=1, device_id={"row": self.row(d)}, device_id_type=MESH)
        for e in range(1, self.nc):
            pl.semaphore_signal(barrier, inc=1, device_id={"col": lax.rem(self.c + e, self.nc)}, device_id_type=MESH)
        peers = self.nr + self.nc - 2
        if waves:
            for n in range(1, self.nw):
                pl.semaphore_signal(barrier, inc=1, device_id=self.wave(n), device_id_type=MESH)
            peers += self.nw - 1
        pl.semaphore_wait(barrier, peers)


def send(src, dst, sems, index, where):
    copy = pltpu.make_async_remote_copy(
        src_ref=src, dst_ref=dst, send_sem=sems.at[(0,) + index], recv_sem=sems.at[(1,) + index],
        device_id=where, device_id_type=MESH)
    copy.start()
    return copy


class Gather:
    def __init__(self, p, full, sems):
        self.p, self.full = p, full
        self.zs, self.bs, self.as_, self.h0, self.h1 = sems
        self.along, self.across, self.relays = {}, {}, {}

    @staticmethod
    def scratch(waves, nr, na, nb):
        return [DMA((2, waves, nr)), DMA((2, waves, nr, nb)), DMA((2, waves, nr, na)), DMA((2, waves, na, nb)), DMA((2, waves, na, nb))]

    def spread(self, w, d):
        p = self.p
        block = self.full.at[w, p.row(p.nr - d) if d else p.r, p.c]
        out = self.across.setdefault(w, [])
        for e in range(1, p.nb):
            out.append(send(block, block, self.bs, (w, d, e), {"col": p.col(0, e)}))
        for f in range(1, p.na):
            out.append(send(block, block, self.as_, (w, d, f), {"col": p.col(f, 0)}))

    def start(self, w):
        p = self.p
        own = self.full.at[w, p.r, p.c]
        self.along[w] = [send(own, own, self.zs, (w, d), {"row": p.row(d)}) for d in range(1, p.nr)]

    def forward(self, w, then=None):
        for d in range(1, self.p.nr):
            self.along[w][d - 1].wait_recv()
            if d == 1 and then is not None:
                then()
            self.spread(w, d)

    def relay(self, w):
        p = self.p
        half = self.full.shape[-1] // 2
        for copy in self.across[w]:
            copy.wait_recv()
        out = self.relays[w] = []
        for e in range(1, p.nb):
            for f in range(1, p.na):
                low = self.full.at[w, :, p.col(0, p.nb - e), :, pl.ds(0, half)]
                out.append(send(low, low, self.h0, (w, f, e), {"col": p.col(f, 0)}))
                top = self.full.at[w, :, p.col(p.na - f, 0), :, pl.ds(half, half)]
                out.append(send(top, top, self.h1, (w, f, e), {"col": p.col(0, e)}))

    def arrive(self, w):
        for copy in self.relays[w]:
            copy.wait_recv()

    def finish(self):
        for groups in (self.along, self.across, self.relays):
            for group in groups.values():
                for copy in group:
                    copy.wait_send()


class Scatter:
    def __init__(self, p, part, scratch):
        self.p, self.part = p, part
        self.g0, self.g1, self.gb, self.ga, self.q, self.gz = scratch[:6]
        self.s0, self.s1, self.db, self.da, self.rb, self.ra, self.zs = scratch[6:]
        self.half = part.shape[-1] // 2
        self.first, self.direct, self.second, self.third = {}, {}, {}, {}

    @staticmethod
    def scratch(waves, nr, na, nb, k, z):
        v = lambda *dims: pltpu.VMEM(dims, f32)
        fa, fb = max(na - 1, 1), max(nb - 1, 1)
        return [
            v(waves, fa, fb, nr, k, z // 2), v(waves, fa, fb, nr, k, z // 2),
            v(waves, fb, nr, k, z), v(waves, fa, nr, k, z), v(waves, nr, k, z), v(waves, nr, k, z),
            DMA((2, waves, na, nb)), DMA((2, waves, na, nb)), DMA((2, waves, nb)), DMA((2, waves, na)),
            DMA((2, waves, nb)), DMA((2, waves, na)), DMA((2, waves, nr))]

    def lanes(self, n):
        return pl.ds(n * self.half, self.half)

    def start(self, w):
        p, out = self.p, []
        for f in range(1, p.na):
            for e in range(1, p.nb):
                diagonal = self.part.at[w, :, p.col(f, e)]
                out.append(send(diagonal.at[:, :, self.lanes(0)], self.g0.at[w, f - 1, e - 1], self.s0, (w, f, e), {"col": p.col(f, 0)}))
                out.append(send(diagonal.at[:, :, self.lanes(1)], self.g1.at[w, f - 1, e - 1], self.s1, (w, f, e), {"col": p.col(0, e)}))
        self.first[w] = out

    def straight(self, w):
        p, out = self.p, []
        low, top = self.lanes(0), self.lanes(1)
        for e in range(1, p.nb):
            out.append(send(self.part.at[w, :, p.col(0, e), :, top], self.gb.at[w, e - 1, :, :, top], self.db, (w, e), {"col": p.col(0, e)}))
        for f in range(1, p.na):
            out.append(send(self.part.at[w, :, p.col(f, 0), :, low], self.ga.at[w, f - 1, :, :, low], self.da, (w, f), {"col": p.col(f, 0)}))
        self.direct[w] = out

    def combine(self, w):
        p, out = self.p, []
        for copy in self.first[w]:
            copy.wait_recv()
        low, top = self.lanes(0), self.lanes(1)
        for e in range(1, p.nb):
            total = self.part[w, :, p.col(0, e), :, low]
            for f in range(1, p.na):
                total = total + self.g0[w, f - 1, e - 1]
            self.g0[w, 0, e - 1] = total
            out.append(send(self.g0.at[w, 0, e - 1], self.gb.at[w, e - 1, :, :, low], self.rb, (w, e), {"col": p.col(0, e)}))
        for f in range(1, p.na):
            total = self.part[w, :, p.col(f, 0), :, top]
            for e in range(1, p.nb):
                total = total + self.g1[w, f - 1, e - 1]
            self.g1[w, f - 1, 0] = total
            out.append(send(self.g1.at[w, f - 1, 0], self.ga.at[w, f - 1, :, :, top], self.ra, (w, f), {"col": p.col(f, 0)}))
        self.second[w] = out

    def column(self, w):
        p, out = self.p, []
        for copy in self.direct[w] + self.second[w]:
            copy.wait_recv()
        total = self.part[w, :, p.c]
        for e in range(1, p.nb):
            total = total + self.gb[w, e - 1]
        for f in range(1, p.na):
            total = total + self.ga[w, f - 1]
        self.q[w] = total
        for d in range(1, p.nr):
            out.append(send(self.q.at[w, p.row(d)], self.gz.at[w, d], self.zs, (w, d), {"row": p.row(d)}))
        self.third[w] = out

    def result(self, w):
        for copy in self.third[w]:
            copy.wait_recv()
        total = self.q[w, self.p.r]
        for d in range(1, self.p.nr):
            total = total + self.gz[w, d]
        return total

    def finish(self):
        for groups in (self.first, self.direct, self.second, self.third):
            for group in groups.values():
                for copy in group:
                    copy.wait_send()

class Halo:
    def __init__(self, p, scratch):
        self.p = p
        self.packed, self.rows, self.cols, self.sems = scratch

    @staticmethod
    def scratch(rows, cols):
        v = lambda *dims: pltpu.VMEM(dims, f32)
        return [v(2, 8, rows), v(2, 8, cols), v(2, 8, rows), DMA((2, 4))]

    def start(self, v):
        p = self.p
        rows, cols = v.shape
        self.packed[0] = jnp.transpose(v[:, 0:128])[0:8]
        self.packed[1] = jnp.transpose(v[:, cols - 128:cols])[120:128]
        up, down = {"row": p.row(p.nr - 1)}, {"row": p.row(1)}
        left, right = {"col": lax.rem(p.c + p.nc - 1, p.nc)}, {"col": lax.rem(p.c + 1, p.nc)}
        self.copies = [
            send(v.at[pl.ds(rows - 8, 8)], self.rows.at[0], self.sems, (0,), down),
            send(v.at[pl.ds(0, 8)], self.rows.at[1], self.sems, (1,), up),
            send(self.packed.at[1], self.cols.at[0], self.sems, (2,), right),
            send(self.packed.at[0], self.cols.at[1], self.sems, (3,), left),
        ]

    def result(self, out_r, out_c):
        p = self.p
        for copy in self.copies:
            copy.wait_recv()
        out_r[0] = jnp.where(p.r > 0, self.rows[0], 0.0)
        out_r[1] = jnp.where(p.r < p.nr - 1, self.rows[1], 0.0)
        out_c[0] = jnp.where(p.c > 0, self.cols[0], 0.0)
        out_c[1] = jnp.where(p.c < p.nc - 1, self.cols[1], 0.0)

    def finish(self):
        for copy in self.copies:
            copy.wait_send()


def curvature(v, i, block, edge_r, edge_c):
    rows = v.shape[0]
    at = pl.multiple_of(i * block, block)
    here = pl.ds(at, block)
    above = v[pl.ds(pl.multiple_of(jnp.maximum(at - 8, 0), 8), 8), :][7:8]
    below = v[pl.ds(pl.multiple_of(jnp.minimum(at + block, rows - 8), 8), 8), :][0:1]
    up = jnp.where(i == 0, edge_r[0, 7:8, :], above)
    down = jnp.where(i == rows // block - 1, edge_r[1, 0:1, :], below)
    return stencil(v[here, :], up, down, column(edge_c[0, 7:8, here]), column(edge_c[1, 0:1, here]))


def curvature_step(dual, ext, edge_r, edge_c, lo, hi):
    def step(i, _):
        here = pl.ds(pl.multiple_of(i * BLOCK, BLOCK), BLOCK)
        moved = dual[here, :] + step_dual * curvature(ext, i, BLOCK, edge_r, edge_c)
        dual[here, :] = prox(moved, curvature_limit)
        return 0

    lax.fori_loop(lo, hi, step, 0)


def split(v):
    top = v.astype(bf16)
    return top, (v - top.astype(f32)).astype(bf16)


def dot3(a, b, over):
    def dot(u, v):
        return lax.dot_general(u, v, (over, ((), ())), preferred_element_type=f32)

    return dot(a[0], b[0]) + dot(a[0], b[1]) + dot(a[1], b[0])


def forward_left(m, w):
    u, cols = m.lh.shape
    step = min(512, cols)
    for n in range(cols // step):
        j = pl.ds(n * step, step)
        m.lh[:, j], m.ll[:, j] = split(dot3((m.rh[w], m.rl[w]), (m.ah[:, j], m.al[:, j]), ((1,), (0,))))


def forward_part(m, w):
    out = dot3((m.lh[...], m.ll[...]), (m.ch[w], m.cl[w]), ((1,), (1,)))
    m.part[w] = out.reshape(m.part.shape[1:])


def back_tile(m, w, t, size):
    rows, cols = m.acc.shape
    i = pl.ds(pl.multiple_of(t * size, size), size)
    s = split(dot3((m.rh[w, :, i], m.rl[w, :, i]), (m.yh[...], m.yl[...]), ((0,), (0,))))
    m.sh[...], m.sl[...] = s
    step = min(512, cols)
    for n in range(cols // step):
        j = pl.ds(n * step, step)
        new = dot3((m.sh[...], m.sl[...]), (m.ch[w, :, j], m.cl[w, :, j]), ((1,), (0,)))
        m.acc[i, j] = new if w == 0 else m.acc[i, j] + new


class Primal:
    def __init__(self, p, m):
        self.p, self.m = p, m
        rows = m.acc.shape[0]
        self.size = m.sh.shape[0]
        self.tiles = rows // self.size
        self.sent = []

    @staticmethod
    def scratch(rows, cols, nw, tile):
        v = lambda *dims: pltpu.VMEM(dims, f32)
        i32 = lambda *dims: pltpu.VMEM(dims, jnp.int32)
        return dict(
            acc=v(rows, cols), other=v(max(nw - 1, 1), rows, cols), wave_sems=DMA((2, rows // tile, nw)),
            x_in=v(2, BLOCK, cols), pupil_in=i32(2, BLOCK, cols), lyot_in=i32(2, BLOCK, cols), in_sems=DMA((2, 3)),
            out_sems=DMA((rows // tile, 4)))

    def load(self, i, slot):
        m = self.m
        here = pl.ds(pl.multiple_of(i * BLOCK, BLOCK), BLOCK)
        pairs = ((m.x, m.x_in), (m.pupil, m.pupil_in), (m.lyot, m.lyot_in))
        return [pltpu.make_async_copy(a.at[here], b.at[slot], m.in_sems.at[slot, n]) for n, (a, b) in enumerate(pairs)]

    def begin(self):
        for i in range(2):
            for copy in self.load(i, i):
                copy.start()

    def exchange(self, t):
        p, m = self.p, self.m
        here = pl.ds(t * self.size, self.size)
        self.sent.append([send(m.acc.at[here], m.other.at[n - 1, here], m.wave_sems, (t, n), p.wave(n)) for n in range(1, p.nw)])

    def step(self, i):
        p, m = self.p, self.m
        slot = lax.rem(i, 2)
        here = pl.ds(pl.multiple_of(i * BLOCK, BLOCK), BLOCK)
        for copy in self.load(i, slot):
            copy.wait()
        pupil = m.pupil_in[slot].astype(f32)
        stop = pupil * m.lyot_in[slot].astype(f32)
        x = m.x_in[slot]
        total = m.acc[here, :]
        for n in range(1, p.nw):
            total = total + m.other[n - 1, here, :]
        gradient = stop * total - pupil + curvature(m.dual_v, i, BLOCK, m.dual_r, m.dual_c)
        new = jnp.clip(x - step_primal * gradient, 0.0, 1.0)
        ext = 2.0 * new - x
        m.acc[here, :] = new
        m.ext_v[here, :] = ext
        m.ah[here, :], m.al[here, :] = split(stop * ext)

        @pl.when(i + 2 < m.acc.shape[0] // BLOCK)
        def _():
            for copy in self.load(i + 2, slot):
                copy.start()

        return 0

    def finish(self):
        m, out = self.m, []
        for t in range(self.tiles):
            for copy in self.sent[t]:
                copy.wait()
            per = self.size // BLOCK
            lax.fori_loop(t * per, (t + 1) * per, lambda i, _: self.step(i), 0)
            here = pl.ds(t * self.size, self.size)
            pairs = ((m.acc, m.x_out), (m.ext_v, m.ext_out), (m.ah, m.ah_out), (m.al, m.al_out))
            for n, (a, b) in enumerate(pairs):
                out.append(pltpu.make_async_copy(a.at[here], b.at[here], m.out_sems.at[t, n]))
                out[-1].start()
        for copy in out:
            copy.wait()


def back_chunk(m, w, gather, primal, between=()):
    gather.arrive(w)
    y = m.full[w].reshape(m.yh.shape)
    m.yh[...], m.yl[...] = split(y)
    last = w == m.full.shape[0] - 1
    if not last and not between:
        lax.fori_loop(0, primal.tiles, lambda t, _: (back_tile(m, w, t, primal.size), 0)[1], 0)
        return
    between = list(between)
    for t in range(primal.tiles):
        back_tile(m, w, t, primal.size)
        if last:
            primal.exchange(t)
        if between:
            between.pop(0)()
    for step in between:
        step()


def back_chunks(m, gather, primal):
    waves = m.full.shape[0]
    steps = {0: [lambda: gather.forward(waves - 1)], 1: [lambda: gather.relay(waves - 2)], 2: [lambda: gather.relay(waves - 1)]}
    if waves < 4:
        gather.forward(waves - 1)
        for w in range(max(waves - 2, 0), waves):
            gather.relay(w)
        steps = {}
    for w in range(waves):
        back_chunk(m, w, gather, primal, steps.get(w, ()))


def first_kernel(m):
    waves = m.full.shape[0]
    p = Place()
    halo, gather, primal = Halo(p, m.halo), Gather(p, m.full, m.gather), Primal(p, m)
    load_dual = pltpu.make_async_copy(m.dual, m.dual_v, m.local.at[0])
    load_dual.start()

    def stage(w):
        return [pltpu.make_async_copy(a.at[w], b.at[w % 2], m.stage_sems.at[w % 2, n])
                for n, (a, b) in enumerate(((m.rows, m.rows_in), (m.cols, m.cols_in)))]

    for w in range(min(2, waves)):
        for copy in stage(w):
            copy.start()
    primal.begin()
    p.greet(True)
    for w in range(waves):
        m.full[w, p.r, p.c] = m.y[:, w, :] * m.dark[:, w, :].astype(f32)
    gather.start(0)
    for w in range(waves):
        gather.spread(w, 0)
    load_dual.wait()
    halo.start(m.dual_v)
    saves = []
    for w in range(waves):
        if w < waves - 1:
            gather.forward(w, lambda: gather.start(w + 1))
        for copy in stage(w):
            copy.wait()
        m.rh[w], m.rl[w] = split(m.rows_in[w % 2])
        m.ch[w], m.cl[w] = split(m.cols_in[w % 2])
        if w + 2 < waves:
            for copy in stage(w + 2):
                copy.start()
        for n, (a, b) in enumerate(((m.rh, m.rh_out), (m.rl, m.rl_out), (m.ch, m.ch_out), (m.cl, m.cl_out))):
            saves.append(pltpu.make_async_copy(a.at[w], b.at[w], m.save_sems.at[w, n]))
            saves[-1].start()
        if 0 < w < waves - 1:
            gather.relay(w - 1)
    halo.result(m.dual_r, m.dual_c)
    back_chunks(m, gather, primal)
    gather.finish()
    halo.finish()
    primal.finish()
    for copy in saves:
        copy.wait()


def turn_kernel(m, again):
    waves = m.part.shape[0]
    p = Place()
    loads = {w: [pltpu.make_async_copy(a.at[w], b.at[w], m.load_sems.at[w, n])
                 for n, (a, b) in enumerate(((m.rh_in, m.rh), (m.rl_in, m.rl), (m.ch_in, m.ch), (m.cl_in, m.cl)))]
             for w in range(waves)}
    pairs = ((m.ah_in, m.ah), (m.al_in, m.al), (m.ext, m.ext_v), (m.dual, m.dual_v))
    local = [pltpu.make_async_copy(a, b, m.local.at[n]) for n, (a, b) in enumerate(pairs)]
    local[0].start()
    local[1].start()
    for w in range(waves):
        for copy in loads[w]:
            copy.start()
        if w == 0:
            local[2].start()
            local[3].start()
    halo, scatter = Halo(p, m.halo), Scatter(p, m.part, m.scatter)
    if again:
        gather, primal, halo2 = Gather(p, m.full, m.gather), Primal(p, m), Halo(p, m.halo2)
    p.greet(again)
    local[0].wait()
    local[1].wait()
    store = pltpu.make_async_copy(m.dual_v, m.dual_out, m.local.at[4])
    blocks = m.ext_v.shape[0] // BLOCK

    def result(w):
        old = m.y[:, w, :]
        dark = m.dark[:, w, :].astype(f32)
        moved = old * dark + step_dual * scatter.result(w)
        new = dark * prox(moved, contrast)
        m.y_out[:, w, :] = new
        if again:
            m.full[w, p.r, p.c] = new
            gather.start(w)
            gather.spread(w, 0)

    def dual(w):
        if w == 0:
            halo.result(m.ext_r, m.ext_c)
            halo.finish()
            local[3].wait()
        curvature_step(m.dual_v, m.ext_v, m.ext_r, m.ext_c, blocks * w // waves, blocks * (w + 1) // waves)
        if w == waves - 1:
            store.start()
            if again:
                halo2.start(m.dual_v)
                primal.begin()

    def steps(*pairs):
        for step, w in pairs:
            if 0 <= w < waves:
                step(w)

    def combine(w):
        scatter.combine(w)
        scatter.straight(w)

    for t in range(waves):
        for copy in loads[t]:
            copy.wait()
        forward_left(m, t)
        steps((combine, t - 1), (scatter.column, t - 2))
        forward_part(m, t)
        scatter.start(t)
        steps((result, t - 3))
        if t == 0:
            local[2].wait()
            halo.start(m.ext_v)
    n = waves
    steps((dual, 0), (result, n - 3), (combine, n - 1), (scatter.column, n - 2))
    if again:
        for w in range(n - 4):
            steps((gather.forward, w), (gather.relay, w))
        steps((gather.forward, n - 4))
    steps((dual, 1), (scatter.column, n - 1), (result, n - 2))
    if again:
        steps((gather.forward, n - 3), (gather.relay, n - 4))
    for w in range(2, waves):
        dual(w)
    steps((result, n - 1))
    if again:
        steps((gather.forward, n - 2), (gather.relay, n - 3))
    scatter.finish()
    if again:
        halo2.result(m.dual_r, m.dual_c)
        halo2.finish()
        back_chunks(m, gather, primal)
        gather.finish()
        primal.finish()
    store.wait()


def call(kernel, ins, outs, scratch, collective_id):
    names, flat, counts = list(ins) + list(outs), [], {}
    for name, what in scratch.items():
        counts[name] = len(what) if isinstance(what, list) else None
        flat += what if isinstance(what, list) else [what]

    def body(*refs):
        m = types.SimpleNamespace(**dict(zip(names, refs)))
        rest = list(refs[len(names):])
        for name, count in counts.items():
            setattr(m, name, [rest.pop(0) for _ in range(count)] if count is not None else rest.pop(0))
        kernel(m)

    out = pl.pallas_call(
        body,
        in_specs=[spec for _, spec in ins.values()], out_specs=[spec for _, spec in outs.values()],
        out_shape=[what for what, _ in outs.values()], scratch_shapes=flat,
        compiler_params=pltpu.CompilerParams(collective_id=collective_id, has_side_effects=True, vmem_limit_bytes=LIMIT),
    )(*[value for value, _ in ins.values()])
    return types.SimpleNamespace(**dict(zip(outs, out)))


def sizes():
    nr, nc, nw = lax.axis_size("row"), lax.axis_size("col"), lax.axis_size("wave")
    na = 2 if nc % 2 == 0 else 1
    return nr, nc, nw, na, nc // na


def common(waves, u, z, rows, cols):
    nr, nc, nw, na, nb = sizes()
    tile = min(512, rows)
    b = lambda *dims: pltpu.VMEM(dims, bf16)
    v = lambda *dims: pltpu.VMEM(dims, f32)
    held = dict(rh=b(waves, u, rows), rl=b(waves, u, rows), ch=b(waves, z, cols), cl=b(waves, z, cols),
                ah=b(rows, cols), al=b(rows, cols), ext_v=v(rows, cols), dual_v=v(rows, cols), local=DMA((5,)), halo=Halo.scratch(rows, cols))
    back = dict(sh=b(tile, z), sl=b(tile, z), yh=b(u, z), yl=b(u, z), dual_r=v(2, 8, cols), dual_c=v(2, 8, rows),
                gather=Gather.scratch(waves, nr, na, nb), **Primal.scratch(rows, cols, nw, tile))
    outs = dict(x_out=(shape(rows, cols), ANY), ext_out=(shape(rows, cols), ANY), ah_out=(shape(rows, cols, kind=bf16), ANY),
                al_out=(shape(rows, cols, kind=bf16), ANY))
    return held, back, outs


def first(y, dark, x, dual, pupil, lyot, focal_rows, focal_cols):
    nr, nc, nw, na, nb = sizes()
    k, waves, z = y.shape
    u = focal_rows.shape[1]
    rows, cols = x.shape
    held, back, outs = common(waves, u, z, rows, cols)
    for name, like in (("rh_out", focal_rows), ("rl_out", focal_rows), ("ch_out", focal_cols), ("cl_out", focal_cols)):
        outs[name] = (shape(*like.shape, kind=bf16), ANY)
    scratch = dict(full=pltpu.VMEM((waves, nr, nc, k, z), f32), rows_in=pltpu.VMEM((2, u, rows), f32), cols_in=pltpu.VMEM((2, z, cols), f32),
                   stage_sems=DMA((2, 2)), save_sems=DMA((waves, 4)), **held, **back)
    ins = dict(y=(y, VMEM), dark=(dark, VMEM), x=(x, ANY), dual=(dual, ANY), pupil=(pupil, ANY), lyot=(lyot, ANY), rows=(focal_rows, ANY), cols=(focal_cols, ANY))
    return call(first_kernel, ins, outs, scratch, 0)


def turn(f, h, y, dark, dual, pupil, lyot, again):
    nr, nc, nw, na, nb = sizes()
    k, waves, z = y.shape
    u = f.rh_out.shape[1]
    rows, cols = dual.shape
    v = lambda *dims: pltpu.VMEM(dims, f32)
    held, back, outs = common(waves, u, z, rows, cols)
    scratch = dict(part=v(waves, nr, nc, k, z), lh=pltpu.VMEM((u, cols), bf16), ll=pltpu.VMEM((u, cols), bf16), load_sems=DMA((waves, 4)),
                   ext_r=v(2, 8, cols), ext_c=v(2, 8, rows), scatter=Scatter.scratch(waves, nr, na, nb, k, z), **held)
    ins = dict(y=(y, VMEM), dark=(dark, VMEM), ext=(h.ext_out, ANY), dual=(dual, ANY), ah_in=(h.ah_out, ANY), al_in=(h.al_out, ANY),
               rh_in=(f.rh_out, ANY), rl_in=(f.rl_out, ANY), ch_in=(f.ch_out, ANY), cl_in=(f.cl_out, ANY))
    ends = dict(y_out=(shape(k, waves, z), VMEM), dual_out=(shape(rows, cols), ANY))
    if again:
        ins.update(x=(h.x_out, ANY), pupil=(pupil, ANY), lyot=(lyot, ANY))
        scratch.update(full=v(waves, nr, nc, k, z), halo2=Halo.scratch(rows, cols), **back)
        ends.update(outs)
    return call(lambda m: turn_kernel(m, again), ins, ends, scratch, 1 if again else 2)


def per_device(transmission, dual_focal, dual_curvature, pupil_mask, lyot_mask, dark_mask, focal_rows, focal_cols):
    y, dual, dark = dual_focal, dual_curvature, dark_mask
    f = h = first(y, dark, transmission, dual, pupil_mask, lyot_mask, focal_rows, focal_cols)
    for iteration in range(ITERS):
        x = h.x_out
        h = turn(f, h, y, dark, dual, pupil_mask, lyot_mask, iteration < ITERS - 1)
        y, dual = h.y_out, h.dual_out
    return x, y, dual


def solution(mesh):
    return jax.shard_map(
        per_device,
        mesh=mesh,
        in_specs=(
            P("row", "col"),
            P(("row", "col"), "wave", None),
            P("row", "col"),
            P("row", "col"),
            P("row", "col"),
            P(("row", "col"), "wave", None),
            P("wave", None, "row"),
            P("wave", None, "col"),
        ),
        out_specs=(P("row", "col"), P(("row", "col"), "wave", None), P("row", "col")),
        check_vma=False,
    )
```

```python
import types

import jax
import jax.numpy as jnp
from jax import lax
from jax.experimental import pallas as pl
from jax.experimental.pallas import tpu as pltpu
from jax.sharding import PartitionSpec as P

ITERS = 2
step_primal = 0.12
step_dual = 0.2
contrast = 0.5
curvature_limit = 0.1
BLOCK = 128
LIMIT = 61 << 20
MESH = pl.DeviceIdType.MESH
f32, bf16 = jnp.float32, jnp.bfloat16
VMEM = pl.BlockSpec(memory_space=pltpu.VMEM)
ANY = pl.BlockSpec(memory_space=pl.ANY)
DMA = pltpu.SemaphoreType.DMA


def shape(*dims, kind=f32):
    return jax.ShapeDtypeStruct(dims, kind)


def prox(v, limit):
    return v - jnp.clip(v, -step_dual * limit, step_dual * limit)


def stencil(v, up, down, left, right):
    rows, cols = v.shape
    r = lax.broadcasted_iota(jnp.int32, v.shape, 0)
    c = lax.broadcasted_iota(jnp.int32, v.shape, 1)
    from_up = jnp.where(r == 0, up, pltpu.roll(v, 1, 0))
    from_down = jnp.where(r == rows - 1, down, pltpu.roll(v, rows - 1, 0))
    from_left = jnp.where(c == 0, left, pltpu.roll(v, 1, 1))
    from_right = jnp.where(c == cols - 1, right, pltpu.roll(v, cols - 1, 1))
    return 0.25 * (from_down + from_up + from_right + from_left) - v


def column(row):
    n = row.shape[1]
    return jnp.transpose(jnp.broadcast_to(row, (128, n)))[:, 0:1]


class Place:
    def __init__(self):
        self.r, self.c = lax.axis_index("row"), lax.axis_index("col")
        self.nr, self.nc = lax.axis_size("row"), lax.axis_size("col")
        self.na = 2 if self.nc % 2 == 0 else 1
        self.nb = self.nc // self.na
        self.w, self.nw = lax.axis_index("wave"), lax.axis_size("wave")
        self.a, self.b = self.c // self.nb, lax.rem(self.c, self.nb)

    def wave(self, n):
        return {"wave": lax.rem(self.w + n, self.nw)}

    def row(self, d):
        return lax.rem(self.r + d, self.nr)

    def col(self, f, e):
        return lax.rem(self.a + f, self.na) * self.nb + lax.rem(self.b + e, self.nb)

    def greet(self, waves):
        barrier = pltpu.get_barrier_semaphore()
        for d in range(1, self.nr):
            pl.semaphore_signal(barrier, inc=1, device_id={"row": self.row(d)}, device_id_type=MESH)
        for e in range(1, self.nc):
            pl.semaphore_signal(barrier, inc=1, device_id={"col": lax.rem(self.c + e, self.nc)}, device_id_type=MESH)
        peers = self.nr + self.nc - 2
        if waves:
            for n in range(1, self.nw):
                pl.semaphore_signal(barrier, inc=1, device_id=self.wave(n), device_id_type=MESH)
            peers += self.nw - 1
        pl.semaphore_wait(barrier, peers)


def remote(src, dst, sems, index, where):
    return pltpu.make_async_remote_copy(
        src_ref=src, dst_ref=dst, send_sem=sems.at[(0,) + index], recv_sem=sems.at[(1,) + index],
        device_id=where, device_id_type=MESH)


def start(copies):
    for copy in copies:
        copy.start()


def arrived(copies):
    for copy in copies:
        copy.wait_recv()


def sent(copies):
    for copy in copies:
        copy.wait_send()


def each(count, step):
    def body(i, carry):
        step(i)
        return carry

    lax.fori_loop(0, count, body, 0)


class Gather:
    def __init__(self, p, full, sems):
        self.p, self.full = p, full
        self.zs, self.bs, self.as_, self.h0, self.h1 = sems

    @staticmethod
    def scratch(waves, nr, na, nb):
        return [DMA((2, waves, nr)), DMA((2, waves, nr, nb)), DMA((2, waves, nr, na)), DMA((2, waves, na, nb)), DMA((2, waves, na, nb))]

    def along(self, w):
        p = self.p
        own = self.full.at[w, p.r, p.c]
        return [remote(own, own, self.zs, (w, d), {"row": p.row(d)}) for d in range(1, p.nr)]

    def across(self, w, d):
        p = self.p
        block = self.full.at[w, p.row(p.nr - d) if d else p.r, p.c]
        return ([remote(block, block, self.bs, (w, d, e), {"col": p.col(0, e)}) for e in range(1, p.nb)]
                + [remote(block, block, self.as_, (w, d, f), {"col": p.col(f, 0)}) for f in range(1, p.na)])

    def relays(self, w):
        p, out = self.p, []
        half = self.full.shape[-1] // 2
        for e in range(1, p.nb):
            for f in range(1, p.na):
                low = self.full.at[w, :, p.col(0, p.nb - e), :, pl.ds(0, half)]
                out.append(remote(low, low, self.h0, (w, f, e), {"col": p.col(f, 0)}))
                top = self.full.at[w, :, p.col(p.na - f, 0), :, pl.ds(half, half)]
                out.append(remote(top, top, self.h1, (w, f, e), {"col": p.col(0, e)}))
        return out

    def start(self, w):
        start(self.along(w))

    def spread(self, w):
        start(self.across(w, 0))

    def forward(self, w, then=None):
        for d, copy in enumerate(self.along(w), 1):
            copy.wait_recv()
            if d == 1 and then is not None:
                then()
            start(self.across(w, d))

    def relay(self, w):
        for d in range(self.p.nr):
            arrived(self.across(w, d))
        start(self.relays(w))

    def arrive(self, w):
        arrived(self.relays(w))

    def finish(self):
        def step(w):
            sent(self.along(w) + self.relays(w))
            for d in range(self.p.nr):
                sent(self.across(w, d))

        each(self.full.shape[0], step)


class Scatter:
    def __init__(self, p, part, scratch):
        self.p, self.part = p, part
        self.g0, self.g1, self.gb, self.ga, self.q, self.gz = scratch[:6]
        self.s0, self.s1, self.db, self.da, self.rb, self.ra, self.zs = scratch[6:]
        half = part.shape[-1] // 2
        self.low, self.top = pl.ds(0, half), pl.ds(half, half)

    @staticmethod
    def scratch(waves, nr, na, nb, k, z):
        v = lambda *dims: pltpu.VMEM(dims, f32)
        fa, fb = max(na - 1, 1), max(nb - 1, 1)
        return [
            v(waves, fa, fb, nr, k, z // 2), v(waves, fa, fb, nr, k, z // 2),
            v(waves, fb, nr, k, z), v(waves, fa, nr, k, z), v(waves, nr, k, z), v(waves, nr, k, z),
            DMA((2, waves, na, nb)), DMA((2, waves, na, nb)), DMA((2, waves, nb)), DMA((2, waves, na)),
            DMA((2, waves, nb)), DMA((2, waves, na)), DMA((2, waves, nr))]

    def first(self, w):
        p, out = self.p, []
        for f in range(1, p.na):
            for e in range(1, p.nb):
                diagonal = self.part.at[w, :, p.col(f, e)]
                out.append(remote(diagonal.at[:, :, self.low], self.g0.at[w, f - 1, e - 1], self.s0, (w, f, e), {"col": p.col(f, 0)}))
                out.append(remote(diagonal.at[:, :, self.top], self.g1.at[w, f - 1, e - 1], self.s1, (w, f, e), {"col": p.col(0, e)}))
        return out

    def direct(self, w):
        p, low, top = self.p, self.low, self.top
        return ([remote(self.part.at[w, :, p.col(0, e), :, top], self.gb.at[w, e - 1, :, :, top], self.db, (w, e), {"col": p.col(0, e)})
                 for e in range(1, p.nb)]
                + [remote(self.part.at[w, :, p.col(f, 0), :, low], self.ga.at[w, f - 1, :, :, low], self.da, (w, f), {"col": p.col(f, 0)})
                   for f in range(1, p.na)])

    def second(self, w):
        p, low, top = self.p, self.low, self.top
        return ([remote(self.g0.at[w, 0, e - 1], self.gb.at[w, e - 1, :, :, low], self.rb, (w, e), {"col": p.col(0, e)})
                 for e in range(1, p.nb)]
                + [remote(self.g1.at[w, f - 1, 0], self.ga.at[w, f - 1, :, :, top], self.ra, (w, f), {"col": p.col(f, 0)})
                   for f in range(1, p.na)])

    def third(self, w):
        p = self.p
        return [remote(self.q.at[w, p.row(d)], self.gz.at[w, d], self.zs, (w, d), {"row": p.row(d)}) for d in range(1, p.nr)]

    def start(self, w):
        start(self.first(w))

    def combine(self, w):
        p = self.p
        arrived(self.first(w))
        for e in range(1, p.nb):
            total = self.part[w, :, p.col(0, e), :, self.low]
            for f in range(1, p.na):
                total = total + self.g0[w, f - 1, e - 1]
            self.g0[w, 0, e - 1] = total
        for f in range(1, p.na):
            total = self.part[w, :, p.col(f, 0), :, self.top]
            for e in range(1, p.nb):
                total = total + self.g1[w, f - 1, e - 1]
            self.g1[w, f - 1, 0] = total
        start(self.second(w) + self.direct(w))

    def column(self, w):
        p = self.p
        arrived(self.direct(w) + self.second(w))
        total = self.part[w, :, p.c]
        for e in range(1, p.nb):
            total = total + self.gb[w, e - 1]
        for f in range(1, p.na):
            total = total + self.ga[w, f - 1]
        self.q[w] = total
        start(self.third(w))

    def result(self, w):
        arrived(self.third(w))
        total = self.q[w, self.p.r]
        for d in range(1, self.p.nr):
            total = total + self.gz[w, d]
        return total

    def finish(self):
        each(self.part.shape[0], lambda w: sent(self.first(w) + self.direct(w) + self.second(w) + self.third(w)))


class Halo:
    def __init__(self, p, v, scratch):
        self.p, self.v = p, v
        self.packed, self.rows, self.cols, self.sems = scratch

    @staticmethod
    def scratch(rows, cols):
        v = lambda *dims: pltpu.VMEM(dims, f32)
        return [v(2, 8, rows), v(2, 8, cols), v(2, 8, rows), DMA((2, 4))]

    def copies(self):
        p, rows = self.p, self.v.shape[0]
        up, down = {"row": p.row(p.nr - 1)}, {"row": p.row(1)}
        left, right = {"col": lax.rem(p.c + p.nc - 1, p.nc)}, {"col": lax.rem(p.c + 1, p.nc)}
        return [
            remote(self.v.at[pl.ds(rows - 8, 8)], self.rows.at[0], self.sems, (0,), down),
            remote(self.v.at[pl.ds(0, 8)], self.rows.at[1], self.sems, (1,), up),
            remote(self.packed.at[1], self.cols.at[0], self.sems, (2,), right),
            remote(self.packed.at[0], self.cols.at[1], self.sems, (3,), left),
        ]

    def start(self):
        cols = self.v.shape[1]
        self.packed[0] = jnp.transpose(self.v[:, 0:128])[0:8]
        self.packed[1] = jnp.transpose(self.v[:, cols - 128:cols])[120:128]
        start(self.copies())

    def result(self, out_r, out_c):
        p = self.p
        arrived(self.copies())
        out_r[0] = jnp.where(p.r > 0, self.rows[0], 0.0)
        out_r[1] = jnp.where(p.r < p.nr - 1, self.rows[1], 0.0)
        out_c[0] = jnp.where(p.c > 0, self.cols[0], 0.0)
        out_c[1] = jnp.where(p.c < p.nc - 1, self.cols[1], 0.0)

    def finish(self):
        sent(self.copies())


def curvature(v, i, block, edge_r, edge_c):
    rows = v.shape[0]
    at = pl.multiple_of(i * block, block)
    here = pl.ds(at, block)
    above = v[pl.ds(pl.multiple_of(jnp.maximum(at - 8, 0), 8), 8), :][7:8]
    below = v[pl.ds(pl.multiple_of(jnp.minimum(at + block, rows - 8), 8), 8), :][0:1]
    up = jnp.where(i == 0, edge_r[0, 7:8, :], above)
    down = jnp.where(i == rows // block - 1, edge_r[1, 0:1, :], below)
    return stencil(v[here, :], up, down, column(edge_c[0, 7:8, here]), column(edge_c[1, 0:1, here]))


def curvature_step(dual, ext, edge_r, edge_c, lo, hi):
    def step(i, _):
        here = pl.ds(pl.multiple_of(i * BLOCK, BLOCK), BLOCK)
        moved = dual[here, :] + step_dual * curvature(ext, i, BLOCK, edge_r, edge_c)
        dual[here, :] = prox(moved, curvature_limit)
        return 0

    lax.fori_loop(lo, hi, step, 0)


def split(v):
    top = v.astype(bf16)
    return top, (v - top.astype(f32)).astype(bf16)


def dot3(a, b, over):
    def dot(u, v):
        return lax.dot_general(u, v, (over, ((), ())), preferred_element_type=f32)

    return dot(a[0], b[0]) + dot(a[0], b[1]) + dot(a[1], b[0])


def forward_left(m, w):
    u, cols = m.lh.shape
    step = min(512, cols)
    for n in range(cols // step):
        j = pl.ds(n * step, step)
        m.lh[:, j], m.ll[:, j] = split(dot3((m.rh[w], m.rl[w]), (m.ah[:, j], m.al[:, j]), ((1,), (0,))))


def forward_part(m, w):
    out = dot3((m.lh[...], m.ll[...]), (m.ch[w], m.cl[w]), ((1,), (1,)))
    m.part[w] = out.reshape(m.part.shape[1:])


def back_tile(m, w, t, size):
    cols = m.acc.shape[1]
    i = pl.ds(pl.multiple_of(t * size, size), size)
    m.sh[...], m.sl[...] = split(dot3((m.rh[w, :, i], m.rl[w, :, i]), (m.yh[...], m.yl[...]), ((0,), (0,))))
    step = min(512, cols)
    for n in range(cols // step):
        j = pl.ds(n * step, step)
        m.acc[i, j] = m.acc[i, j] + dot3((m.sh[...], m.sl[...]), (m.ch[w, :, j], m.cl[w, :, j]), ((1,), (0,)))


def clear(m):
    def step(i):
        m.acc[pl.ds(pl.multiple_of(i * BLOCK, BLOCK), BLOCK), :] = jnp.zeros((BLOCK, m.acc.shape[1]), f32)

    each(m.acc.shape[0] // BLOCK, step)


class Primal:
    def __init__(self, p, m, x, x_out):
        self.p, self.m, self.x, self.x_out = p, m, x, x_out
        rows = m.acc.shape[0]
        self.size = m.sh.shape[0]
        self.tiles = rows // self.size

    @staticmethod
    def scratch(rows, cols, nw, tile):
        v = lambda *dims: pltpu.VMEM(dims, f32)
        i32 = lambda *dims: pltpu.VMEM(dims, jnp.int32)
        return dict(
            acc=v(rows, cols), other=v(max(nw - 1, 1), rows, cols), wave_sems=DMA((2, rows // tile, nw)),
            x_in=v(2, BLOCK, cols), pupil_in=i32(2, BLOCK, cols), lyot_in=i32(2, BLOCK, cols), in_sems=DMA((2, 3)),
            out_sems=DMA((rows // tile,)))

    def load(self, i, slot):
        m = self.m
        here = pl.ds(pl.multiple_of(i * BLOCK, BLOCK), BLOCK)
        pairs = ((self.x, m.x_in), (m.pupil, m.pupil_in), (m.lyot, m.lyot_in))
        return [pltpu.make_async_copy(a.at[here], b.at[slot], m.in_sems.at[slot, n]) for n, (a, b) in enumerate(pairs)]

    def begin(self):
        for i in range(2):
            for copy in self.load(i, i):
                copy.start()

    def exchange(self, t):
        p, m = self.p, self.m
        here = pl.ds(pl.multiple_of(t * self.size, self.size), self.size)
        return [remote(m.acc.at[here], m.other.at[n - 1, here], m.wave_sems, (t, n), p.wave(n)) for n in range(1, p.nw)]

    def store(self, t):
        m = self.m
        here = pl.ds(pl.multiple_of(t * self.size, self.size), self.size)
        return pltpu.make_async_copy(m.acc.at[here], self.x_out.at[here], m.out_sems.at[t])

    def step(self, i):
        p, m = self.p, self.m
        slot = lax.rem(i, 2)
        here = pl.ds(pl.multiple_of(i * BLOCK, BLOCK), BLOCK)
        for copy in self.load(i, slot):
            copy.wait()
        pupil = m.pupil_in[slot].astype(f32)
        stop = pupil * m.lyot_in[slot].astype(f32)
        x = m.x_in[slot]
        total = m.acc[here, :]
        for n in range(1, p.nw):
            total = total + m.other[n - 1, here, :]
        gradient = stop * total - pupil + curvature(m.dual_v, i, BLOCK, m.dual_r, m.dual_c)
        new = jnp.clip(x - step_primal * gradient, 0.0, 1.0)
        ext = 2.0 * new - x
        m.acc[here, :] = new
        m.ext_v[here, :] = ext
        m.ah[here, :], m.al[here, :] = split(stop * ext)

        @pl.when(i + 2 < m.acc.shape[0] // BLOCK)
        def _():
            for copy in self.load(i + 2, slot):
                copy.start()

    def finish(self):
        per = self.size // BLOCK

        def tile(t):
            for copy in self.exchange(t):
                copy.wait()
            each(per, lambda i: self.step(t * per + i))
            self.store(t).start()

        each(self.tiles, tile)

    def stored(self):
        each(self.tiles, lambda t: self.store(t).wait())


def back_chunks(m, gather, primal, wait_free):
    waves = m.full.shape[0]
    late = waves >= 4
    if not late:
        gather.forward(waves - 1)
        for w in range(max(waves - 2, 0), waves):
            gather.relay(w)

    def give(t):
        if wait_free:
            @pl.when(t == 0)
            def _():
                pl.semaphore_wait(m.free, primal.p.nw - 1)
        start(primal.exchange(t))

    def chunk(w):
        gather.arrive(w)
        m.yh[...], m.yl[...] = split(m.full[w].reshape(m.yh.shape))

        def tile(t):
            back_tile(m, w, t, primal.size)
            if late:
                pl.when((w == 0) & (t == 0))(lambda: gather.forward(waves - 1))
                pl.when((w == 1) & (t == 0))(lambda: gather.relay(waves - 2))
                pl.when((w == 2) & (t == 0))(lambda: gather.relay(waves - 1))
            pl.when(w == waves - 1)(lambda: give(t))

        each(primal.tiles, tile)

    each(waves, chunk)


def kernel(m):
    waves, u = m.full.shape[0], m.rh.shape[1]
    rows, cols = m.acc.shape
    blocks, slots = rows // BLOCK, max(1, min(2, rows // u))
    p = Place()
    gather, scatter = Gather(p, m.full, m.gather), Scatter(p, m.part, m.scatter)
    load_dual = pltpu.make_async_copy(m.dual, m.dual_v, m.local.at[0])
    load_dual.start()

    def stage(w):
        here = pl.ds(pl.multiple_of(lax.rem(w, slots) * u, u), u) if slots > 1 else pl.ds(0, u)
        return [pltpu.make_async_copy(a.at[w], b.at[here], m.stage_sems.at[w, n])
                for n, (a, b) in enumerate(((m.focal_rows, m.ext_v), (m.focal_cols, m.acc)))]

    def convert(w):
        for copy in stage(w):
            copy.wait()
        base = lax.rem(w, slots) * u
        for a, top, low in ((m.ext_v, m.rh, m.rl), (m.acc, m.ch, m.cl)):
            def part(i):
                here = pl.ds(pl.multiple_of(i * 64, 64), 64)
                top[w, here, :], low[w, here, :] = split(a[pl.ds(pl.multiple_of(base + i * 64, 64), 64), :])

            each(u // 64, part)
        pl.when(w + slots < waves)(lambda: start(stage(w + slots)))

    each(slots, lambda w: start(stage(w)))
    p.greet(True)
    for w in range(waves):
        m.full[w, p.r, p.c] = m.y[:, w, :] * m.dark[:, w, :].astype(f32)
    gather.start(0)
    for w in range(waves):
        gather.spread(w)
    halo = Halo(p, m.dual_v, m.halos[:4])
    load_dual.wait()
    halo.start()

    def advance(w):
        pl.when(w < waves - 1)(lambda: gather.forward(w, lambda: gather.start(w + 1)))
        convert(w)
        pl.when((w > 0) & (w < waves - 1))(lambda: gather.relay(w - 1))

    each(waves, advance)
    clear(m)
    halo.result(m.dual_r, m.dual_c)
    halo.finish()
    for iteration in range(ITERS):
        first, last = iteration == 0, iteration == ITERS - 1
        primal = Primal(p, m, m.x if first else m.x_mid, m.x_out if last else m.x_mid)
        primal.begin()
        back_chunks(m, gather, primal, not first)
        gather.finish()
        primal.finish()
        if not last:
            for n in range(1, p.nw):
                pl.semaphore_signal(m.free, inc=1, device_id=p.wave(n), device_id_type=MESH)
        forward_and_turn(m, p, gather, scatter, 1 + 2 * iteration, primal, first, last)


def forward_and_turn(m, p, gather, scatter, halos, primal, first, last):
    n = m.full.shape[0]
    blocks = m.ext_v.shape[0] // BLOCK
    halo = Halo(p, m.ext_v, m.halos[4 * halos:4 * halos + 4])
    halo.start()

    def result(w):
        dark = m.dark[:, w, :].astype(f32)
        old = m.y[:, w, :] * dark if first else m.y_out[:, w, :]
        new = dark * prox(old + step_dual * scatter.result(w), contrast)
        m.y_out[:, w, :] = new
        if not last:
            m.full[w, p.r, p.c] = new
            gather.start(w)
            gather.spread(w)

    def dual(lo, hi):
        curvature_step(m.dual_v, m.ext_v, m.ext_r, m.ext_c, blocks * lo // 4, blocks * hi // 4)

    def steps(*pairs):
        for step, w in pairs:
            if 0 <= w < n:
                step(w)

    def product(w):
        forward_left(m, w)
        pl.when(w >= 1)(lambda: scatter.combine(w - 1))
        pl.when(w >= 2)(lambda: scatter.column(w - 2))
        forward_part(m, w)
        scatter.start(w)

    each(n, product)
    for w in range(n - 3):
        result(w)
    halo.result(m.ext_r, m.ext_c)
    halo.finish()
    primal.stored()
    if not last:
        clear(m)
    dual(0, 1)
    steps((result, n - 3), (scatter.combine, n - 1), (scatter.column, n - 2))
    if not last:
        for w in range(n - 4):
            steps((gather.forward, w), (gather.relay, w))
        steps((gather.forward, n - 4))
    dual(1, 2)
    steps((scatter.column, n - 1), (result, n - 2))
    if not last:
        steps((gather.forward, n - 3), (gather.relay, n - 4))
    dual(2, 4)
    if last:
        store = pltpu.make_async_copy(m.dual_v, m.dual_out, m.local.at[1])
        store.start()
    else:
        halo = Halo(p, m.dual_v, m.halos[4 * halos + 4:4 * halos + 8])
        halo.start()
    steps((result, n - 1))
    if not last:
        steps((gather.forward, n - 2), (gather.relay, n - 3))
    scatter.finish()
    if last:
        store.wait()
    else:
        halo.result(m.dual_r, m.dual_c)
        halo.finish()


def call(ins, outs, scratch):
    names, flat, counts = list(ins) + list(outs), [], {}
    for name, what in scratch.items():
        counts[name] = len(what) if isinstance(what, list) else None
        flat += what if isinstance(what, list) else [what]

    def body(*refs):
        m = types.SimpleNamespace(**dict(zip(names, refs)))
        rest = list(refs[len(names):])
        for name, count in counts.items():
            setattr(m, name, [rest.pop(0) for _ in range(count)] if count is not None else rest.pop(0))
        kernel(m)

    out = pl.pallas_call(
        body,
        in_specs=[spec for _, spec in ins.values()], out_specs=[spec for _, spec in outs.values()],
        out_shape=[what for what, _ in outs.values()], scratch_shapes=flat,
        compiler_params=pltpu.CompilerParams(collective_id=0, has_side_effects=True, vmem_limit_bytes=LIMIT),
    )(*[value for value, _ in ins.values()])
    return types.SimpleNamespace(**dict(zip(outs, out)))


def per_device(transmission, dual_focal, dual_curvature, pupil_mask, lyot_mask, dark_mask, focal_rows, focal_cols):
    nr, nc, nw = lax.axis_size("row"), lax.axis_size("col"), lax.axis_size("wave")
    na = 2 if nc % 2 == 0 else 1
    nb = nc // na
    k, waves, z = dual_focal.shape
    u = focal_rows.shape[1]
    rows, cols = transmission.shape
    tile = min(512, rows)
    assert rows == cols and u <= rows and u == z, "tile shape"
    b = lambda *dims: pltpu.VMEM(dims, bf16)
    v = lambda *dims: pltpu.VMEM(dims, f32)
    scratch = dict(
        rh=b(waves, u, rows), rl=b(waves, u, rows), ch=b(waves, z, cols), cl=b(waves, z, cols), stage_sems=DMA((waves, 2)),
        ah=b(rows, cols), al=b(rows, cols), ext_v=v(rows, cols), dual_v=v(rows, cols), local=DMA((2,)),
        full=v(waves, nr, nc, k, z), part=v(waves, nr, nc, k, z), lh=b(u, cols), ll=b(u, cols), sh=b(tile, z), sl=b(tile, z),
        yh=b(u, z), yl=b(u, z), dual_r=v(2, 8, cols), dual_c=v(2, 8, rows), ext_r=v(2, 8, cols), ext_c=v(2, 8, rows),
        free=pltpu.SemaphoreType.REGULAR, gather=Gather.scratch(waves, nr, na, nb), scatter=Scatter.scratch(waves, nr, na, nb, k, z),
        halos=Halo.scratch(rows, cols) * (2 * ITERS), **Primal.scratch(rows, cols, nw, tile))
    ins = dict(
        y=(dual_focal, VMEM), dark=(dark_mask, VMEM), x=(transmission, ANY), dual=(dual_curvature, ANY), pupil=(pupil_mask, ANY),
        lyot=(lyot_mask, ANY), focal_rows=(focal_rows, ANY), focal_cols=(focal_cols, ANY))
    outs = dict(
        x_out=(shape(rows, cols), ANY), y_out=(shape(k, waves, z), VMEM), dual_out=(shape(rows, cols), ANY), x_mid=(shape(rows, cols), ANY))
    out = call(ins, outs, scratch)
    return out.x_out, out.y_out, out.dual_out


def solution(mesh):
    return jax.shard_map(
        per_device,
        mesh=mesh,
        in_specs=(
            P("row", "col"),
            P(("row", "col"), "wave", None),
            P("row", "col"),
            P("row", "col"),
            P("row", "col"),
            P(("row", "col"), "wave", None),
            P("wave", None, "row"),
            P("wave", None, "col"),
        ),
        out_specs=(P("row", "col"), P(("row", "col"), "wave", None), P("row", "col")),
        check_vma=False,
    )
```

```python
import types

import jax
import jax.numpy as jnp
from jax import lax
from jax.experimental import pallas as pl
from jax.experimental.pallas import tpu as pltpu
from jax.sharding import PartitionSpec as P

ITERS = 2
step_primal = 0.12
step_dual = 0.2
contrast = 0.5
curvature_limit = 0.1
BLOCK = 128
LIMIT = 61 << 20
MESH = pl.DeviceIdType.MESH
f32, bf16 = jnp.float32, jnp.bfloat16
VMEM = pl.BlockSpec(memory_space=pltpu.VMEM)
ANY = pl.BlockSpec(memory_space=pl.ANY)
DMA = pltpu.SemaphoreType.DMA


def shape(*dims, kind=f32):
    return jax.ShapeDtypeStruct(dims, kind)


def prox(v, limit):
    return v - jnp.clip(v, -step_dual * limit, step_dual * limit)


def stencil(v, up, down, left, right):
    rows, cols = v.shape
    r = lax.broadcasted_iota(jnp.int32, v.shape, 0)
    c = lax.broadcasted_iota(jnp.int32, v.shape, 1)
    from_up = jnp.where(r == 0, up, pltpu.roll(v, 1, 0))
    from_down = jnp.where(r == rows - 1, down, pltpu.roll(v, rows - 1, 0))
    from_left = jnp.where(c == 0, left, pltpu.roll(v, 1, 1))
    from_right = jnp.where(c == cols - 1, right, pltpu.roll(v, cols - 1, 1))
    return 0.25 * (from_down + from_up + from_right + from_left) - v


def column(row):
    n = row.shape[1]
    return jnp.transpose(jnp.broadcast_to(row, (128, n)))[:, 0:1]


class Place:
    def __init__(self):
        self.r, self.c = lax.axis_index("row"), lax.axis_index("col")
        self.nr, self.nc = lax.axis_size("row"), lax.axis_size("col")
        self.na = 2 if self.nc % 2 == 0 else 1
        self.nb = self.nc // self.na
        self.w, self.nw = lax.axis_index("wave"), lax.axis_size("wave")
        self.a, self.b = self.c // self.nb, lax.rem(self.c, self.nb)

    def wave(self, n):
        return {"wave": lax.rem(self.w + n, self.nw)}

    def row(self, d):
        return lax.rem(self.r + d, self.nr)

    def col(self, f, e):
        return lax.rem(self.a + f, self.na) * self.nb + lax.rem(self.b + e, self.nb)

    def greet(self, waves):
        barrier = pltpu.get_barrier_semaphore()
        for d in range(1, self.nr):
            pl.semaphore_signal(barrier, inc=1, device_id={"row": self.row(d)}, device_id_type=MESH)
        for e in range(1, self.nc):
            pl.semaphore_signal(barrier, inc=1, device_id={"col": lax.rem(self.c + e, self.nc)}, device_id_type=MESH)
        peers = self.nr + self.nc - 2
        if waves:
            for n in range(1, self.nw):
                pl.semaphore_signal(barrier, inc=1, device_id=self.wave(n), device_id_type=MESH)
            peers += self.nw - 1
        pl.semaphore_wait(barrier, peers)


def remote(src, dst, sems, index, where):
    return pltpu.make_async_remote_copy(
        src_ref=src, dst_ref=dst, send_sem=sems.at[(0,) + index], recv_sem=sems.at[(1,) + index],
        device_id=where, device_id_type=MESH)


def start(copies):
    for copy in copies:
        copy.start()


def arrived(copies):
    for copy in copies:
        copy.wait_recv()


def sent(copies):
    for copy in copies:
        copy.wait_send()


def each(count, step):
    def body(i, carry):
        step(i)
        return carry

    lax.fori_loop(0, count, body, 0)


class Gather:
    def __init__(self, p, full, sems):
        self.p, self.full = p, full
        self.zs, self.bs, self.as_, self.h0, self.h1 = sems

    @staticmethod
    def scratch(waves, nr, na, nb):
        return [DMA((2, waves, nr)), DMA((2, waves, nr, nb)), DMA((2, waves, nr, na)), DMA((2, waves, na, nb)), DMA((2, waves, na, nb))]

    def along(self, w):
        p = self.p
        own = self.full.at[w, p.r, p.c]
        return [remote(own, own, self.zs, (w, d), {"row": p.row(d)}) for d in range(1, p.nr)]

    def across(self, w, d):
        p = self.p
        block = self.full.at[w, p.row(p.nr - d) if d else p.r, p.c]
        return ([remote(block, block, self.bs, (w, d, e), {"col": p.col(0, e)}) for e in range(1, p.nb)]
                + [remote(block, block, self.as_, (w, d, f), {"col": p.col(f, 0)}) for f in range(1, p.na)])

    def relays(self, w):
        p, out = self.p, []
        half = self.full.shape[-1] // 2
        for e in range(1, p.nb):
            for f in range(1, p.na):
                low = self.full.at[w, :, p.col(0, p.nb - e), :, pl.ds(0, half)]
                out.append(remote(low, low, self.h0, (w, f, e), {"col": p.col(f, 0)}))
                top = self.full.at[w, :, p.col(p.na - f, 0), :, pl.ds(half, half)]
                out.append(remote(top, top, self.h1, (w, f, e), {"col": p.col(0, e)}))
        return out

    def start(self, w):
        start(self.along(w))

    def spread(self, w):
        start(self.across(w, 0))

    def forward(self, w, then=None):
        for d, copy in enumerate(self.along(w), 1):
            copy.wait_recv()
            if d == 1 and then is not None:
                then()
            start(self.across(w, d))

    def relay(self, w):
        for d in range(self.p.nr):
            arrived(self.across(w, d))
        start(self.relays(w))

    def arrive(self, w):
        arrived(self.relays(w))

    def finish(self):
        def step(w):
            sent(self.along(w) + self.relays(w))
            for d in range(self.p.nr):
                sent(self.across(w, d))

        each(self.full.shape[0], step)


class Scatter:
    def __init__(self, p, part, scratch):
        self.p, self.part = p, part
        self.g0, self.g1, self.gb, self.ga, self.q, self.gz = scratch[:6]
        self.s0, self.s1, self.db, self.da, self.rb, self.ra, self.zs = scratch[6:]
        half = part.shape[-1] // 2
        self.low, self.top = pl.ds(0, half), pl.ds(half, half)

    @staticmethod
    def scratch(waves, nr, na, nb, k, z):
        v = lambda *dims: pltpu.VMEM(dims, f32)
        fa, fb = max(na - 1, 1), max(nb - 1, 1)
        return [
            v(waves, fa, fb, nr, k, z // 2), v(waves, fa, fb, nr, k, z // 2),
            v(waves, fb, nr, k, z), v(waves, fa, nr, k, z), v(waves, nr, k, z), v(waves, nr, k, z),
            DMA((2, waves, na, nb)), DMA((2, waves, na, nb)), DMA((2, waves, nb)), DMA((2, waves, na)),
            DMA((2, waves, nb)), DMA((2, waves, na)), DMA((2, waves, nr))]

    def first(self, w):
        p, out = self.p, []
        for f in range(1, p.na):
            for e in range(1, p.nb):
                diagonal = self.part.at[w, :, p.col(f, e)]
                out.append(remote(diagonal.at[:, :, self.low], self.g0.at[w, f - 1, e - 1], self.s0, (w, f, e), {"col": p.col(f, 0)}))
                out.append(remote(diagonal.at[:, :, self.top], self.g1.at[w, f - 1, e - 1], self.s1, (w, f, e), {"col": p.col(0, e)}))
        return out

    def direct(self, w):
        p, low, top = self.p, self.low, self.top
        return ([remote(self.part.at[w, :, p.col(0, e), :, top], self.gb.at[w, e - 1, :, :, top], self.db, (w, e), {"col": p.col(0, e)})
                 for e in range(1, p.nb)]
                + [remote(self.part.at[w, :, p.col(f, 0), :, low], self.ga.at[w, f - 1, :, :, low], self.da, (w, f), {"col": p.col(f, 0)})
                   for f in range(1, p.na)])

    def second(self, w):
        p, low, top = self.p, self.low, self.top
        return ([remote(self.g0.at[w, 0, e - 1], self.gb.at[w, e - 1, :, :, low], self.rb, (w, e), {"col": p.col(0, e)})
                 for e in range(1, p.nb)]
                + [remote(self.g1.at[w, f - 1, 0], self.ga.at[w, f - 1, :, :, top], self.ra, (w, f), {"col": p.col(f, 0)})
                   for f in range(1, p.na)])

    def third(self, w):
        p = self.p
        return [remote(self.q.at[w, p.row(d)], self.gz.at[w, d], self.zs, (w, d), {"row": p.row(d)}) for d in range(1, p.nr)]

    def start(self, w):
        start(self.first(w))

    def combine(self, w):
        p = self.p
        arrived(self.first(w))
        for e in range(1, p.nb):
            total = self.part[w, :, p.col(0, e), :, self.low]
            for f in range(1, p.na):
                total = total + self.g0[w, f - 1, e - 1]
            self.g0[w, 0, e - 1] = total
        for f in range(1, p.na):
            total = self.part[w, :, p.col(f, 0), :, self.top]
            for e in range(1, p.nb):
                total = total + self.g1[w, f - 1, e - 1]
            self.g1[w, f - 1, 0] = total
        start(self.second(w) + self.direct(w))

    def column(self, w):
        p = self.p
        arrived(self.direct(w) + self.second(w))
        total = self.part[w, :, p.c]
        for e in range(1, p.nb):
            total = total + self.gb[w, e - 1]
        for f in range(1, p.na):
            total = total + self.ga[w, f - 1]
        self.q[w] = total
        start(self.third(w))

    def result(self, w):
        arrived(self.third(w))
        total = self.q[w, self.p.r]
        for d in range(1, self.p.nr):
            total = total + self.gz[w, d]
        return total

    def finish(self):
        each(self.part.shape[0], lambda w: sent(self.first(w) + self.direct(w) + self.second(w) + self.third(w)))


class Halo:
    def __init__(self, p, v, scratch):
        self.p, self.v = p, v
        self.packed, self.rows, self.cols, self.sems = scratch

    @staticmethod
    def scratch(rows, cols):
        v = lambda *dims: pltpu.VMEM(dims, f32)
        return [v(2, 8, rows), v(2, 8, cols), v(2, 8, rows), DMA((2, 4))]

    def copies(self):
        p, rows = self.p, self.v.shape[0]
        up, down = {"row": p.row(p.nr - 1)}, {"row": p.row(1)}
        left, right = {"col": lax.rem(p.c + p.nc - 1, p.nc)}, {"col": lax.rem(p.c + 1, p.nc)}
        return [
            remote(self.v.at[pl.ds(rows - 8, 8)], self.rows.at[0], self.sems, (0,), down),
            remote(self.v.at[pl.ds(0, 8)], self.rows.at[1], self.sems, (1,), up),
            remote(self.packed.at[1], self.cols.at[0], self.sems, (2,), right),
            remote(self.packed.at[0], self.cols.at[1], self.sems, (3,), left),
        ]

    def start(self):
        cols = self.v.shape[1]
        self.packed[0] = jnp.transpose(self.v[:, 0:128])[0:8]
        self.packed[1] = jnp.transpose(self.v[:, cols - 128:cols])[120:128]
        start(self.copies())

    def result(self, out_r, out_c):
        p = self.p
        arrived(self.copies())
        out_r[0] = jnp.where(p.r > 0, self.rows[0], 0.0)
        out_r[1] = jnp.where(p.r < p.nr - 1, self.rows[1], 0.0)
        out_c[0] = jnp.where(p.c > 0, self.cols[0], 0.0)
        out_c[1] = jnp.where(p.c < p.nc - 1, self.cols[1], 0.0)

    def finish(self):
        sent(self.copies())


def curvature(v, i, block, edge_r, edge_c):
    rows = v.shape[0]
    at = pl.multiple_of(i * block, block)
    here = pl.ds(at, block)
    above = v[pl.ds(pl.multiple_of(jnp.maximum(at - 8, 0), 8), 8), :][7:8]
    below = v[pl.ds(pl.multiple_of(jnp.minimum(at + block, rows - 8), 8), 8), :][0:1]
    up = jnp.where(i == 0, edge_r[0, 7:8, :], above)
    down = jnp.where(i == rows // block - 1, edge_r[1, 0:1, :], below)
    return stencil(v[here, :], up, down, column(edge_c[0, 7:8, here]), column(edge_c[1, 0:1, here]))


def curvature_step(dual, ext, edge_r, edge_c, lo, hi):
    def step(i, _):
        here = pl.ds(pl.multiple_of(i * BLOCK, BLOCK), BLOCK)
        moved = dual[here, :] + step_dual * curvature(ext, i, BLOCK, edge_r, edge_c)
        dual[here, :] = prox(moved, curvature_limit)
        return 0

    lax.fori_loop(lo, hi, step, 0)


def split(v):
    top = v.astype(bf16)
    return top, (v - top.astype(f32)).astype(bf16)


def dot3(a, b, over):
    def dot(u, v):
        return lax.dot_general(u, v, (over, ((), ())), preferred_element_type=f32)

    return dot(a[0], b[0]) + dot(a[0], b[1]) + dot(a[1], b[0])


def forward_left(m, w):
    u, cols = m.lh.shape
    step = min(512, cols)
    for n in range(cols // step):
        j = pl.ds(n * step, step)
        m.lh[:, j], m.ll[:, j] = split(dot3((m.rh[w], m.rl[w]), (m.ah[:, j], m.al[:, j]), ((1,), (0,))))


def forward_part(m, w):
    out = dot3((m.lh[...], m.ll[...]), (m.ch[w], m.cl[w]), ((1,), (1,)))
    m.part[w] = out.reshape(m.part.shape[1:])


def back_tile(m, w, t, size, then):
    cols = m.acc.shape[1]
    i = pl.ds(pl.multiple_of(t * size, size), size)
    m.sh[...], m.sl[...] = split(dot3((m.rh[w, :, i], m.rl[w, :, i]), (m.yh[...], m.yl[...]), ((0,), (0,))))
    step = min(512, cols)
    for n in range(cols // step):
        j = pl.ds(n * step, step)
        m.acc[i, j] = m.acc[i, j] + dot3((m.sh[...], m.sl[...]), (m.ch[w, :, j], m.cl[w, :, j]), ((1,), (0,)))
        then(n)


def clear(m):
    def step(i):
        m.acc[pl.ds(pl.multiple_of(i * BLOCK, BLOCK), BLOCK), :] = jnp.zeros((BLOCK, m.acc.shape[1]), f32)

    each(m.acc.shape[0] // BLOCK, step)


class Primal:
    def __init__(self, p, m, x, x_out):
        self.p, self.m, self.x, self.x_out = p, m, x, x_out
        self.width = min(512, m.acc.shape[1])
        self.pieces = m.acc.shape[1] // self.width
        rows = m.acc.shape[0]
        self.size = m.sh.shape[0]
        self.tiles = rows // self.size

    @staticmethod
    def scratch(rows, cols, nw, tile):
        v = lambda *dims: pltpu.VMEM(dims, f32)
        i32 = lambda *dims: pltpu.VMEM(dims, jnp.int32)
        return dict(
            acc=v(rows, cols), other=v(max(nw - 1, 1), rows, cols), wave_sems=DMA((2, rows // tile, nw, cols // min(512, cols))),
            x_in=v(2, BLOCK, cols), pupil_in=i32(2, BLOCK, cols), lyot_in=i32(2, BLOCK, cols), in_sems=DMA((2, 3)),
            out_sems=DMA((rows // tile,)))

    def load(self, i, slot):
        m = self.m
        here = pl.ds(pl.multiple_of(i * BLOCK, BLOCK), BLOCK)
        pairs = ((self.x, m.x_in), (m.pupil, m.pupil_in), (m.lyot, m.lyot_in))
        return [pltpu.make_async_copy(a.at[here], b.at[slot], m.in_sems.at[slot, n]) for n, (a, b) in enumerate(pairs)]

    def begin(self):
        for i in range(2):
            for copy in self.load(i, i):
                copy.start()

    def exchange(self, t, n):
        p, m = self.p, self.m
        here = pl.ds(pl.multiple_of(t * self.size, self.size), self.size), pl.ds(n * self.width, self.width)
        return [remote(m.acc.at[here], m.other.at[(e - 1,) + here], m.wave_sems, (t, e, n), p.wave(e)) for e in range(1, p.nw)]

    def store(self, t):
        m = self.m
        here = pl.ds(pl.multiple_of(t * self.size, self.size), self.size)
        return pltpu.make_async_copy(m.acc.at[here], self.x_out.at[here], m.out_sems.at[t])

    def step(self, i):
        p, m = self.p, self.m
        slot = lax.rem(i, 2)
        here = pl.ds(pl.multiple_of(i * BLOCK, BLOCK), BLOCK)
        for copy in self.load(i, slot):
            copy.wait()
        pupil = m.pupil_in[slot].astype(f32)
        stop = pupil * m.lyot_in[slot].astype(f32)
        x = m.x_in[slot]
        total = m.acc[here, :]
        for n in range(1, p.nw):
            total = total + m.other[n - 1, here, :]
        gradient = stop * total - pupil + curvature(m.dual_v, i, BLOCK, m.dual_r, m.dual_c)
        new = jnp.clip(x - step_primal * gradient, 0.0, 1.0)
        ext = 2.0 * new - x
        m.acc[here, :] = new
        m.ext_v[here, :] = ext
        m.ah[here, :], m.al[here, :] = split(stop * ext)

        @pl.when(i + 2 < m.acc.shape[0] // BLOCK)
        def _():
            for copy in self.load(i + 2, slot):
                copy.start()

    def finish(self):
        per = self.size // BLOCK

        def tile(t):
            for n in range(self.pieces):
                for copy in self.exchange(t, n):
                    copy.wait()
            each(per, lambda i: self.step(t * per + i))
            self.store(t).start()

        each(self.tiles, tile)

    def stored(self):
        each(self.tiles, lambda t: self.store(t).wait())


def back_chunks(m, gather, primal, wait_free):
    waves = m.full.shape[0]
    late = waves >= 4
    if not late:
        gather.forward(waves - 1)
        for w in range(max(waves - 2, 0), waves):
            gather.relay(w)

    def give(t, n):
        if wait_free and n == 0:
            @pl.when(t == 0)
            def _():
                pl.semaphore_wait(m.free, primal.p.nw - 1)
        start(primal.exchange(t, n))

    def chunk(w):
        gather.arrive(w)
        m.yh[...], m.yl[...] = split(m.full[w].reshape(m.yh.shape))

        def tile(t):
            back_tile(m, w, t, primal.size, lambda n: pl.when(w == waves - 1)(lambda: give(t, n)))
            if late:
                pl.when((w == 0) & (t == 0))(lambda: gather.forward(waves - 1))
                pl.when((w == 1) & (t == 0))(lambda: gather.relay(waves - 2))
                pl.when((w == 2) & (t == 0))(lambda: gather.relay(waves - 1))

        each(primal.tiles, tile)

    each(waves, chunk)


def kernel(m):
    waves, u = m.full.shape[0], m.rh.shape[1]
    rows, cols = m.acc.shape
    blocks, slots = rows // BLOCK, max(1, min(2, rows // u))
    p = Place()
    gather, scatter = Gather(p, m.full, m.gather), Scatter(p, m.part, m.scatter)
    load_dual = pltpu.make_async_copy(m.dual, m.dual_v, m.local.at[0])
    load_dual.start()

    def stage(w):
        here = pl.ds(pl.multiple_of(lax.rem(w, slots) * u, u), u) if slots > 1 else pl.ds(0, u)
        return [pltpu.make_async_copy(a.at[w], b.at[here], m.stage_sems.at[w, n])
                for n, (a, b) in enumerate(((m.focal_rows, m.ext_v), (m.focal_cols, m.acc)))]

    def convert(w):
        for copy in stage(w):
            copy.wait()
        base = lax.rem(w, slots) * u
        for a, top, low in ((m.ext_v, m.rh, m.rl), (m.acc, m.ch, m.cl)):
            def part(i):
                here = pl.ds(pl.multiple_of(i * 64, 64), 64)
                top[w, here, :], low[w, here, :] = split(a[pl.ds(pl.multiple_of(base + i * 64, 64), 64), :])

            each(u // 64, part)
        pl.when(w + slots < waves)(lambda: start(stage(w + slots)))

    each(slots, lambda w: start(stage(w)))
    p.greet(True)
    for w in range(waves):
        m.full[w, p.r, p.c] = m.y[:, w, :] * m.dark[:, w, :].astype(f32)
    gather.start(0)
    for w in range(waves):
        gather.spread(w)
    halo = Halo(p, m.dual_v, m.halos[:4])
    load_dual.wait()
    halo.start()

    def advance(w):
        pl.when(w < waves - 1)(lambda: gather.forward(w, lambda: gather.start(w + 1)))
        convert(w)
        pl.when((w > 0) & (w < waves - 1))(lambda: gather.relay(w - 1))

    each(waves, advance)
    clear(m)
    halo.result(m.dual_r, m.dual_c)
    halo.finish()
    for iteration in range(ITERS):
        first, last = iteration == 0, iteration == ITERS - 1
        primal = Primal(p, m, m.x if first else m.x_mid, m.x_out if last else m.x_mid)
        primal.begin()
        back_chunks(m, gather, primal, not first)
        gather.finish()
        primal.finish()
        if not last:
            for n in range(1, p.nw):
                pl.semaphore_signal(m.free, inc=1, device_id=p.wave(n), device_id_type=MESH)
        forward_and_turn(m, p, gather, scatter, 1 + 2 * iteration, primal, first, last)


def forward_and_turn(m, p, gather, scatter, halos, primal, first, last):
    n = m.full.shape[0]
    blocks = m.ext_v.shape[0] // BLOCK
    halo = Halo(p, m.ext_v, m.halos[4 * halos:4 * halos + 4])
    halo.start()

    def result(w):
        dark = m.dark[:, w, :].astype(f32)
        old = m.y[:, w, :] * dark if first else m.y_out[:, w, :]
        new = dark * prox(old + step_dual * scatter.result(w), contrast)
        m.y_out[:, w, :] = new
        if not last:
            m.full[w, p.r, p.c] = new
            gather.start(w)
            gather.spread(w)

    def dual(lo, hi):
        curvature_step(m.dual_v, m.ext_v, m.ext_r, m.ext_c, blocks * lo // 4, blocks * hi // 4)

    def steps(*pairs):
        for step, w in pairs:
            if 0 <= w < n:
                step(w)

    def product(w):
        forward_left(m, w)
        pl.when(w >= 1)(lambda: scatter.combine(w - 1))
        pl.when(w >= 2)(lambda: scatter.column(w - 2))
        forward_part(m, w)
        scatter.start(w)

    each(n, product)
    for w in range(n - 3):
        result(w)
    halo.result(m.ext_r, m.ext_c)
    halo.finish()
    primal.stored()
    if not last:
        clear(m)
    dual(0, 1)
    steps((result, n - 3), (scatter.combine, n - 1), (scatter.column, n - 2))
    if not last:
        for w in range(n - 4):
            steps((gather.forward, w), (gather.relay, w))
        steps((gather.forward, n - 4))
    dual(1, 2)
    steps((scatter.column, n - 1), (result, n - 2))
    if not last:
        steps((gather.forward, n - 3), (gather.relay, n - 4))
    dual(2, 4)
    if last:
        store = pltpu.make_async_copy(m.dual_v, m.dual_out, m.local.at[1])
        store.start()
    else:
        halo = Halo(p, m.dual_v, m.halos[4 * halos + 4:4 * halos + 8])
        halo.start()
    steps((result, n - 1))
    if not last:
        steps((gather.forward, n - 2), (gather.relay, n - 3))
    scatter.finish()
    if last:
        store.wait()
    else:
        halo.result(m.dual_r, m.dual_c)
        halo.finish()


def call(ins, outs, scratch):
    names, flat, counts = list(ins) + list(outs), [], {}
    for name, what in scratch.items():
        counts[name] = len(what) if isinstance(what, list) else None
        flat += what if isinstance(what, list) else [what]

    def body(*refs):
        m = types.SimpleNamespace(**dict(zip(names, refs)))
        rest = list(refs[len(names):])
        for name, count in counts.items():
            setattr(m, name, [rest.pop(0) for _ in range(count)] if count is not None else rest.pop(0))
        kernel(m)

    out = pl.pallas_call(
        body,
        in_specs=[spec for _, spec in ins.values()], out_specs=[spec for _, spec in outs.values()],
        out_shape=[what for what, _ in outs.values()], scratch_shapes=flat,
        compiler_params=pltpu.CompilerParams(collective_id=0, has_side_effects=True, vmem_limit_bytes=LIMIT),
    )(*[value for value, _ in ins.values()])
    return types.SimpleNamespace(**dict(zip(outs, out)))


def per_device(transmission, dual_focal, dual_curvature, pupil_mask, lyot_mask, dark_mask, focal_rows, focal_cols):
    nr, nc, nw = lax.axis_size("row"), lax.axis_size("col"), lax.axis_size("wave")
    na = 2 if nc % 2 == 0 else 1
    nb = nc // na
    k, waves, z = dual_focal.shape
    u = focal_rows.shape[1]
    rows, cols = transmission.shape
    tile = min(512, rows)
    assert rows == cols and u <= rows and u == z, "tile shape"
    b = lambda *dims: pltpu.VMEM(dims, bf16)
    v = lambda *dims: pltpu.VMEM(dims, f32)
    scratch = dict(
        rh=b(waves, u, rows), rl=b(waves, u, rows), ch=b(waves, z, cols), cl=b(waves, z, cols), stage_sems=DMA((waves, 2)),
        ah=b(rows, cols), al=b(rows, cols), ext_v=v(rows, cols), dual_v=v(rows, cols), local=DMA((2,)),
        full=v(waves, nr, nc, k, z), part=v(waves, nr, nc, k, z), lh=b(u, cols), ll=b(u, cols), sh=b(tile, z), sl=b(tile, z),
        yh=b(u, z), yl=b(u, z), dual_r=v(2, 8, cols), dual_c=v(2, 8, rows), ext_r=v(2, 8, cols), ext_c=v(2, 8, rows),
        free=pltpu.SemaphoreType.REGULAR, gather=Gather.scratch(waves, nr, na, nb), scatter=Scatter.scratch(waves, nr, na, nb, k, z),
        halos=Halo.scratch(rows, cols) * (2 * ITERS), **Primal.scratch(rows, cols, nw, tile))
    ins = dict(
        y=(dual_focal, VMEM), dark=(dark_mask, VMEM), x=(transmission, ANY), dual=(dual_curvature, ANY), pupil=(pupil_mask, ANY),
        lyot=(lyot_mask, ANY), focal_rows=(focal_rows, ANY), focal_cols=(focal_cols, ANY))
    outs = dict(
        x_out=(shape(rows, cols), ANY), y_out=(shape(k, waves, z), VMEM), dual_out=(shape(rows, cols), ANY), x_mid=(shape(rows, cols), ANY))
    out = call(ins, outs, scratch)
    return out.x_out, out.y_out, out.dual_out


def solution(mesh):
    return jax.shard_map(
        per_device,
        mesh=mesh,
        in_specs=(
            P("row", "col"),
            P(("row", "col"), "wave", None),
            P("row", "col"),
            P("row", "col"),
            P("row", "col"),
            P(("row", "col"), "wave", None),
            P("wave", None, "row"),
            P("wave", None, "col"),
        ),
        out_specs=(P("row", "col"), P(("row", "col"), "wave", None), P("row", "col")),
        check_vma=False,
    )
```

```python
import types

import jax
import jax.numpy as jnp
from jax import lax
from jax.experimental import pallas as pl
from jax.experimental.pallas import tpu as pltpu
from jax.sharding import PartitionSpec as P

ITERS = 2
step_primal = 0.12
step_dual = 0.2
contrast = 0.5
curvature_limit = 0.1
BLOCK = 128
LIMIT = 61 << 20
MESH = pl.DeviceIdType.MESH
f32, bf16 = jnp.float32, jnp.bfloat16
VMEM = pl.BlockSpec(memory_space=pltpu.VMEM)
ANY = pl.BlockSpec(memory_space=pl.ANY)
DMA = pltpu.SemaphoreType.DMA


def shape(*dims, kind=f32):
    return jax.ShapeDtypeStruct(dims, kind)


def prox(v, limit):
    return v - jnp.clip(v, -step_dual * limit, step_dual * limit)


def stencil(v, up, down, left, right):
    rows, cols = v.shape
    r = lax.broadcasted_iota(jnp.int32, v.shape, 0)
    c = lax.broadcasted_iota(jnp.int32, v.shape, 1)
    from_up = jnp.where(r == 0, up, pltpu.roll(v, 1, 0))
    from_down = jnp.where(r == rows - 1, down, pltpu.roll(v, rows - 1, 0))
    from_left = jnp.where(c == 0, left, pltpu.roll(v, 1, 1))
    from_right = jnp.where(c == cols - 1, right, pltpu.roll(v, cols - 1, 1))
    return 0.25 * (from_down + from_up + from_right + from_left) - v


def column(row):
    n = row.shape[1]
    return jnp.transpose(jnp.broadcast_to(row, (128, n)))[:, 0:1]


class Place:
    def __init__(self):
        self.r, self.c = lax.axis_index("row"), lax.axis_index("col")
        self.nr, self.nc = lax.axis_size("row"), lax.axis_size("col")
        self.na = 2 if self.nc % 2 == 0 else 1
        self.nb = self.nc // self.na
        self.w, self.nw = lax.axis_index("wave"), lax.axis_size("wave")
        self.a, self.b = self.c // self.nb, lax.rem(self.c, self.nb)

    def wave(self, n):
        return {"wave": lax.rem(self.w + n, self.nw)}

    def row(self, d):
        return lax.rem(self.r + d, self.nr)

    def col(self, f, e):
        return lax.rem(self.a + f, self.na) * self.nb + lax.rem(self.b + e, self.nb)

    def greet(self, waves):
        barrier = pltpu.get_barrier_semaphore()
        for d in range(1, self.nr):
            pl.semaphore_signal(barrier, inc=1, device_id={"row": self.row(d)}, device_id_type=MESH)
        for e in range(1, self.nc):
            pl.semaphore_signal(barrier, inc=1, device_id={"col": lax.rem(self.c + e, self.nc)}, device_id_type=MESH)
        peers = self.nr + self.nc - 2
        if waves:
            for n in range(1, self.nw):
                pl.semaphore_signal(barrier, inc=1, device_id=self.wave(n), device_id_type=MESH)
            peers += self.nw - 1
        pl.semaphore_wait(barrier, peers)


def remote(src, dst, sems, index, where):
    return pltpu.make_async_remote_copy(
        src_ref=src, dst_ref=dst, send_sem=sems.at[(0,) + index], recv_sem=sems.at[(1,) + index],
        device_id=where, device_id_type=MESH)


def start(copies):
    for copy in copies:
        copy.start()


def arrived(copies):
    for copy in copies:
        copy.wait_recv()


def sent(copies):
    for copy in copies:
        copy.wait_send()


def each(count, step):
    def body(i, carry):
        step(i)
        return carry

    lax.fori_loop(0, count, body, 0)


class Gather:
    def __init__(self, p, full, sems):
        self.p, self.full = p, full
        self.zs, self.bs, self.as_, self.h0, self.h1 = sems

    @staticmethod
    def scratch(waves, nr, na, nb):
        return [DMA((2, waves, nr)), DMA((2, waves, nr, nb)), DMA((2, waves, nr, na)), DMA((2, waves, na, nb)), DMA((2, waves, na, nb))]

    def along(self, w):
        p = self.p
        own = self.full.at[w, p.r, p.c]
        return [remote(own, own, self.zs, (w, d), {"row": p.row(d)}) for d in range(1, p.nr)]

    def across(self, w, d):
        p = self.p
        block = self.full.at[w, p.row(p.nr - d) if d else p.r, p.c]
        return ([remote(block, block, self.bs, (w, d, e), {"col": p.col(0, e)}) for e in range(1, p.nb)]
                + [remote(block, block, self.as_, (w, d, f), {"col": p.col(f, 0)}) for f in range(1, p.na)])

    def relays(self, w):
        p, out = self.p, []
        half = self.full.shape[-1] // 2
        for e in range(1, p.nb):
            for f in range(1, p.na):
                low = self.full.at[w, :, p.col(0, p.nb - e), :, pl.ds(0, half)]
                out.append(remote(low, low, self.h0, (w, f, e), {"col": p.col(f, 0)}))
                top = self.full.at[w, :, p.col(p.na - f, 0), :, pl.ds(half, half)]
                out.append(remote(top, top, self.h1, (w, f, e), {"col": p.col(0, e)}))
        return out

    def start(self, w):
        start(self.along(w))

    def spread(self, w):
        start(self.across(w, 0))

    def forward(self, w, then=None):
        for d, copy in enumerate(self.along(w), 1):
            copy.wait_recv()
            if d == 1 and then is not None:
                then()
            start(self.across(w, d))

    def relay(self, w):
        for d in range(self.p.nr):
            arrived(self.across(w, d))
        start(self.relays(w))

    def arrive(self, w):
        arrived(self.relays(w))

    def finish(self):
        def step(w):
            sent(self.along(w) + self.relays(w))
            for d in range(self.p.nr):
                sent(self.across(w, d))

        each(self.full.shape[0], step)


class Scatter:
    def __init__(self, p, part, scratch):
        self.p, self.part = p, part
        self.g0, self.g1, self.gb, self.ga, self.q, self.gz = scratch[:6]
        self.s0, self.s1, self.db, self.da, self.rb, self.ra, self.zs = scratch[6:]
        half = part.shape[-1] // 2
        self.low, self.top = pl.ds(0, half), pl.ds(half, half)

    @staticmethod
    def scratch(waves, nr, na, nb, k, z):
        v = lambda *dims: pltpu.VMEM(dims, f32)
        fa, fb = max(na - 1, 1), max(nb - 1, 1)
        return [
            v(waves, fa, fb, nr, k, z // 2), v(waves, fa, fb, nr, k, z // 2),
            v(waves, fb, nr, k, z), v(waves, fa, nr, k, z), v(waves, nr, k, z), v(waves, nr, k, z),
            DMA((2, waves, na, nb)), DMA((2, waves, na, nb)), DMA((2, waves, nb)), DMA((2, waves, na)),
            DMA((2, waves, nb)), DMA((2, waves, na)), DMA((2, waves, nr))]

    def first(self, w):
        p, out = self.p, []
        for f in range(1, p.na):
            for e in range(1, p.nb):
                diagonal = self.part.at[w, :, p.col(f, e)]
                out.append(remote(diagonal.at[:, :, self.low], self.g0.at[w, f - 1, e - 1], self.s0, (w, f, e), {"col": p.col(f, 0)}))
                out.append(remote(diagonal.at[:, :, self.top], self.g1.at[w, f - 1, e - 1], self.s1, (w, f, e), {"col": p.col(0, e)}))
        return out

    def direct(self, w):
        p, low, top = self.p, self.low, self.top
        return ([remote(self.part.at[w, :, p.col(0, e), :, top], self.gb.at[w, e - 1, :, :, top], self.db, (w, e), {"col": p.col(0, e)})
                 for e in range(1, p.nb)]
                + [remote(self.part.at[w, :, p.col(f, 0), :, low], self.ga.at[w, f - 1, :, :, low], self.da, (w, f), {"col": p.col(f, 0)})
                   for f in range(1, p.na)])

    def second(self, w):
        p, low, top = self.p, self.low, self.top
        return ([remote(self.g0.at[w, 0, e - 1], self.gb.at[w, e - 1, :, :, low], self.rb, (w, e), {"col": p.col(0, e)})
                 for e in range(1, p.nb)]
                + [remote(self.g1.at[w, f - 1, 0], self.ga.at[w, f - 1, :, :, top], self.ra, (w, f), {"col": p.col(f, 0)})
                   for f in range(1, p.na)])

    def third(self, w):
        p = self.p
        return [remote(self.q.at[w, p.row(d)], self.gz.at[w, d], self.zs, (w, d), {"row": p.row(d)}) for d in range(1, p.nr)]

    def start(self, w):
        start(self.first(w) + self.direct(w))

    def combine(self, w):
        p = self.p
        arrived(self.first(w))
        for e in range(1, p.nb):
            total = self.part[w, :, p.col(0, e), :, self.low]
            for f in range(1, p.na):
                total = total + self.g0[w, f - 1, e - 1]
            self.g0[w, 0, e - 1] = total
        for f in range(1, p.na):
            total = self.part[w, :, p.col(f, 0), :, self.top]
            for e in range(1, p.nb):
                total = total + self.g1[w, f - 1, e - 1]
            self.g1[w, f - 1, 0] = total
        start(self.second(w))

    def column(self, w):
        p = self.p
        arrived(self.direct(w) + self.second(w))
        total = self.part[w, :, p.c]
        for e in range(1, p.nb):
            total = total + self.gb[w, e - 1]
        for f in range(1, p.na):
            total = total + self.ga[w, f - 1]
        self.q[w] = total
        start(self.third(w))

    def result(self, w):
        arrived(self.third(w))
        total = self.q[w, self.p.r]
        for d in range(1, self.p.nr):
            total = total + self.gz[w, d]
        return total

    def finish(self):
        each(self.part.shape[0], lambda w: sent(self.first(w) + self.direct(w) + self.second(w) + self.third(w)))


class Halo:
    def __init__(self, p, v, scratch):
        self.p, self.v = p, v
        self.packed, self.rows, self.cols, self.sems = scratch

    @staticmethod
    def scratch(rows, cols):
        v = lambda *dims: pltpu.VMEM(dims, f32)
        return [v(2, 8, rows), v(2, 8, cols), v(2, 8, rows), DMA((2, 4))]

    def copies(self):
        p, rows = self.p, self.v.shape[0]
        up, down = {"row": p.row(p.nr - 1)}, {"row": p.row(1)}
        left, right = {"col": lax.rem(p.c + p.nc - 1, p.nc)}, {"col": lax.rem(p.c + 1, p.nc)}
        return [
            remote(self.v.at[pl.ds(rows - 8, 8)], self.rows.at[0], self.sems, (0,), down),
            remote(self.v.at[pl.ds(0, 8)], self.rows.at[1], self.sems, (1,), up),
            remote(self.packed.at[1], self.cols.at[0], self.sems, (2,), right),
            remote(self.packed.at[0], self.cols.at[1], self.sems, (3,), left),
        ]

    def start(self):
        cols = self.v.shape[1]
        self.packed[0] = jnp.transpose(self.v[:, 0:128])[0:8]
        self.packed[1] = jnp.transpose(self.v[:, cols - 128:cols])[120:128]
        start(self.copies())

    def result(self, out_r, out_c):
        p = self.p
        arrived(self.copies())
        out_r[0] = jnp.where(p.r > 0, self.rows[0], 0.0)
        out_r[1] = jnp.where(p.r < p.nr - 1, self.rows[1], 0.0)
        out_c[0] = jnp.where(p.c > 0, self.cols[0], 0.0)
        out_c[1] = jnp.where(p.c < p.nc - 1, self.cols[1], 0.0)

    def finish(self):
        sent(self.copies())


def curvature(v, i, block, edge_r, edge_c):
    rows = v.shape[0]
    at = pl.multiple_of(i * block, block)
    here = pl.ds(at, block)
    above = v[pl.ds(pl.multiple_of(jnp.maximum(at - 8, 0), 8), 8), :][7:8]
    below = v[pl.ds(pl.multiple_of(jnp.minimum(at + block, rows - 8), 8), 8), :][0:1]
    up = jnp.where(i == 0, edge_r[0, 7:8, :], above)
    down = jnp.where(i == rows // block - 1, edge_r[1, 0:1, :], below)
    return stencil(v[here, :], up, down, column(edge_c[0, 7:8, here]), column(edge_c[1, 0:1, here]))


def curvature_step(dual, ext, edge_r, edge_c, lo, hi):
    def step(i, _):
        here = pl.ds(pl.multiple_of(i * BLOCK, BLOCK), BLOCK)
        moved = dual[here, :] + step_dual * curvature(ext, i, BLOCK, edge_r, edge_c)
        dual[here, :] = prox(moved, curvature_limit)
        return 0

    lax.fori_loop(lo, hi, step, 0)


def split(v):
    top = v.astype(bf16)
    return top, (v - top.astype(f32)).astype(bf16)


def dot3(a, b, over):
    def dot(u, v):
        return lax.dot_general(u, v, (over, ((), ())), preferred_element_type=f32)

    return dot(a[0], b[0]) + dot(a[0], b[1]) + dot(a[1], b[0])


def forward_left(m, w):
    u, cols = m.lh.shape
    step = min(512, cols)
    for n in range(cols // step):
        j = pl.ds(n * step, step)
        m.lh[:, j], m.ll[:, j] = split(dot3((m.rh[w], m.rl[w]), (m.ah[:, j], m.al[:, j]), ((1,), (0,))))


def forward_part(m, w):
    out = dot3((m.lh[...], m.ll[...]), (m.ch[w], m.cl[w]), ((1,), (1,)))
    m.part[w] = out.reshape(m.part.shape[1:])


def back_tile(m, w, t, size, then):
    cols = m.acc.shape[1]
    i = pl.ds(pl.multiple_of(t * size, size), size)
    m.sh[...], m.sl[...] = split(dot3((m.rh[w, :, i], m.rl[w, :, i]), (m.yh[...], m.yl[...]), ((0,), (0,))))
    step = min(512, cols)
    for n in range(cols // step):
        j = pl.ds(n * step, step)
        m.acc[i, j] = m.acc[i, j] + dot3((m.sh[...], m.sl[...]), (m.ch[w, :, j], m.cl[w, :, j]), ((1,), (0,)))
        then(n)


def clear(m):
    def step(i):
        m.acc[pl.ds(pl.multiple_of(i * BLOCK, BLOCK), BLOCK), :] = jnp.zeros((BLOCK, m.acc.shape[1]), f32)

    each(m.acc.shape[0] // BLOCK, step)


class Primal:
    def __init__(self, p, m, x, x_out):
        self.p, self.m, self.x, self.x_out = p, m, x, x_out
        self.width = min(512, m.acc.shape[1])
        self.pieces = m.acc.shape[1] // self.width
        rows = m.acc.shape[0]
        self.size = m.sh.shape[0]
        self.tiles = rows // self.size

    @staticmethod
    def scratch(rows, cols, nw, tile):
        v = lambda *dims: pltpu.VMEM(dims, f32)
        i32 = lambda *dims: pltpu.VMEM(dims, jnp.int32)
        return dict(
            acc=v(rows, cols), other=v(max(nw - 1, 1), rows, cols), wave_sems=DMA((2, rows // tile, nw, cols // min(512, cols))),
            x_in=v(2, BLOCK, cols), pupil_in=i32(2, BLOCK, cols), lyot_in=i32(2, BLOCK, cols), in_sems=DMA((2, 3)),
            out_sems=DMA((rows // tile,)))

    def load(self, i, slot):
        m = self.m
        here = pl.ds(pl.multiple_of(i * BLOCK, BLOCK), BLOCK)
        pairs = ((self.x, m.x_in), (m.pupil, m.pupil_in), (m.lyot, m.lyot_in))
        return [pltpu.make_async_copy(a.at[here], b.at[slot], m.in_sems.at[slot, n]) for n, (a, b) in enumerate(pairs)]

    def begin(self):
        for i in range(2):
            for copy in self.load(i, i):
                copy.start()

    def exchange(self, t, n):
        p, m = self.p, self.m
        here = pl.ds(pl.multiple_of(t * self.size, self.size), self.size), pl.ds(n * self.width, self.width)
        return [remote(m.acc.at[here], m.other.at[(e - 1,) + here], m.wave_sems, (t, e, n), p.wave(e)) for e in range(1, p.nw)]

    def store(self, t):
        m = self.m
        here = pl.ds(pl.multiple_of(t * self.size, self.size), self.size)
        return pltpu.make_async_copy(m.acc.at[here], self.x_out.at[here], m.out_sems.at[t])

    def step(self, i):
        p, m = self.p, self.m
        slot = lax.rem(i, 2)
        here = pl.ds(pl.multiple_of(i * BLOCK, BLOCK), BLOCK)
        for copy in self.load(i, slot):
            copy.wait()
        pupil = m.pupil_in[slot].astype(f32)
        stop = pupil * m.lyot_in[slot].astype(f32)
        x = m.x_in[slot]
        total = m.acc[here, :]
        for n in range(1, p.nw):
            total = total + m.other[n - 1, here, :]
        gradient = stop * total - pupil + curvature(m.dual_v, i, BLOCK, m.dual_r, m.dual_c)
        new = jnp.clip(x - step_primal * gradient, 0.0, 1.0)
        ext = 2.0 * new - x
        m.acc[here, :] = new
        m.ext_v[here, :] = ext
        m.ah[here, :], m.al[here, :] = split(stop * ext)

        @pl.when(i + 2 < m.acc.shape[0] // BLOCK)
        def _():
            for copy in self.load(i + 2, slot):
                copy.start()

    def finish(self):
        per = self.size // BLOCK

        def tile(t):
            for n in range(self.pieces):
                for copy in self.exchange(t, n):
                    copy.wait()
            each(per, lambda i: self.step(t * per + i))
            self.store(t).start()

        each(self.tiles, tile)

    def stored(self):
        each(self.tiles, lambda t: self.store(t).wait())


def back_chunks(m, gather, primal, wait_free):
    waves = m.full.shape[0]
    late = waves >= 4
    if not late:
        gather.forward(waves - 1)
        for w in range(max(waves - 2, 0), waves):
            gather.relay(w)

    def give(t, n):
        if wait_free and n == 0:
            @pl.when(t == 0)
            def _():
                pl.semaphore_wait(m.free, primal.p.nw - 1)
        start(primal.exchange(t, n))

    def chunk(w):
        gather.arrive(w)
        m.yh[...], m.yl[...] = split(m.full[w].reshape(m.yh.shape))

        def tile(t):
            back_tile(m, w, t, primal.size, lambda n: pl.when(w == waves - 1)(lambda: give(t, n)))
            if late:
                pl.when((w == 0) & (t == 0))(lambda: gather.forward(waves - 1))
                pl.when((w == 1) & (t == 0))(lambda: gather.relay(waves - 2))
                pl.when((w == 2) & (t == 0))(lambda: gather.relay(waves - 1))

        each(primal.tiles, tile)

    each(waves, chunk)


def kernel(m):
    waves, u = m.full.shape[0], m.rh.shape[1]
    rows, cols = m.acc.shape
    blocks, slots = rows // BLOCK, max(1, min(2, rows // u))
    p = Place()
    gather, scatter = Gather(p, m.full, m.gather), Scatter(p, m.part, m.scatter)
    load_dual = pltpu.make_async_copy(m.dual, m.dual_v, m.local.at[0])
    load_dual.start()

    def stage(w):
        here = pl.ds(pl.multiple_of(lax.rem(w, slots) * u, u), u) if slots > 1 else pl.ds(0, u)
        return [pltpu.make_async_copy(a.at[w], b.at[here], m.stage_sems.at[w, n])
                for n, (a, b) in enumerate(((m.focal_rows, m.ext_v), (m.focal_cols, m.acc)))]

    def convert(w):
        for copy in stage(w):
            copy.wait()
        base = lax.rem(w, slots) * u
        for a, top, low in ((m.ext_v, m.rh, m.rl), (m.acc, m.ch, m.cl)):
            def part(i):
                here = pl.ds(pl.multiple_of(i * 64, 64), 64)
                top[w, here, :], low[w, here, :] = split(a[pl.ds(pl.multiple_of(base + i * 64, 64), 64), :])

            each(u // 64, part)
        pl.when(w + slots < waves)(lambda: start(stage(w + slots)))

    each(slots, lambda w: start(stage(w)))
    for w in range(waves):
        m.full[w, p.r, p.c] = m.y[:, w, :] * m.dark[:, w, :].astype(f32)
    p.greet(True)
    gather.start(0)
    for w in range(waves):
        gather.spread(w)
    halo = Halo(p, m.dual_v, m.halos[:4])
    load_dual.wait()
    halo.start()

    def advance(w):
        pl.when(w < waves - 1)(lambda: gather.forward(w, lambda: gather.start(w + 1)))
        convert(w)
        pl.when((w > 0) & (w < waves - 1))(lambda: gather.relay(w - 1))

    each(waves, advance)
    clear(m)
    halo.result(m.dual_r, m.dual_c)
    halo.finish()
    for iteration in range(ITERS):
        first, last = iteration == 0, iteration == ITERS - 1
        primal = Primal(p, m, m.x if first else m.x_mid, m.x_out if last else m.x_mid)
        primal.begin()
        back_chunks(m, gather, primal, not first)
        gather.finish()
        primal.finish()
        if not last:
            for n in range(1, p.nw):
                pl.semaphore_signal(m.free, inc=1, device_id=p.wave(n), device_id_type=MESH)
        forward_and_turn(m, p, gather, scatter, 1 + 2 * iteration, primal, first, last)


def forward_and_turn(m, p, gather, scatter, halos, primal, first, last):
    n = m.full.shape[0]
    blocks = m.ext_v.shape[0] // BLOCK
    halo = Halo(p, m.ext_v, m.halos[4 * halos:4 * halos + 4])
    halo.start()

    def result(w):
        dark = m.dark[:, w, :].astype(f32)
        old = m.y[:, w, :] * dark if first else m.y_out[:, w, :]
        new = dark * prox(old + step_dual * scatter.result(w), contrast)
        m.y_out[:, w, :] = new
        if not last:
            m.full[w, p.r, p.c] = new
            gather.start(w)
            gather.spread(w)

    def dual(lo, hi):
        curvature_step(m.dual_v, m.ext_v, m.ext_r, m.ext_c, blocks * lo // 4, blocks * hi // 4)

    def steps(*pairs):
        for step, w in pairs:
            if 0 <= w < n:
                step(w)

    def product(w):
        forward_left(m, w)
        pl.when(w >= 1)(lambda: scatter.combine(w - 1))
        forward_part(m, w)
        scatter.start(w)
        pl.when(w >= 2)(lambda: scatter.column(w - 2))

    each(n, product)
    for w in range(n - 3):
        result(w)
    halo.result(m.ext_r, m.ext_c)
    halo.finish()
    primal.stored()
    if not last:
        clear(m)
    dual(0, 1)
    steps((result, n - 3), (scatter.combine, n - 1), (scatter.column, n - 2))
    if not last:
        for w in range(n - 4):
            steps((gather.forward, w), (gather.relay, w))
        steps((gather.forward, n - 4))
    dual(1, 2)
    steps((scatter.column, n - 1), (result, n - 2))
    if not last:
        steps((gather.forward, n - 3), (gather.relay, n - 4))
    dual(2, 4)
    if last:
        store = pltpu.make_async_copy(m.dual_v, m.dual_out, m.local.at[1])
        store.start()
    else:
        halo = Halo(p, m.dual_v, m.halos[4 * halos + 4:4 * halos + 8])
        halo.start()
    steps((result, n - 1))
    if not last:
        steps((gather.forward, n - 2), (gather.relay, n - 3))
    scatter.finish()
    if last:
        store.wait()
    else:
        halo.result(m.dual_r, m.dual_c)
        halo.finish()


def call(ins, outs, scratch):
    names, flat, counts = list(ins) + list(outs), [], {}
    for name, what in scratch.items():
        counts[name] = len(what) if isinstance(what, list) else None
        flat += what if isinstance(what, list) else [what]

    def body(*refs):
        m = types.SimpleNamespace(**dict(zip(names, refs)))
        rest = list(refs[len(names):])
        for name, count in counts.items():
            setattr(m, name, [rest.pop(0) for _ in range(count)] if count is not None else rest.pop(0))
        kernel(m)

    out = pl.pallas_call(
        body,
        in_specs=[spec for _, spec in ins.values()], out_specs=[spec for _, spec in outs.values()],
        out_shape=[what for what, _ in outs.values()], scratch_shapes=flat,
        compiler_params=pltpu.CompilerParams(collective_id=0, has_side_effects=True, vmem_limit_bytes=LIMIT),
    )(*[value for value, _ in ins.values()])
    return types.SimpleNamespace(**dict(zip(outs, out)))


def per_device(transmission, dual_focal, dual_curvature, pupil_mask, lyot_mask, dark_mask, focal_rows, focal_cols):
    nr, nc, nw = lax.axis_size("row"), lax.axis_size("col"), lax.axis_size("wave")
    na = 2 if nc % 2 == 0 else 1
    nb = nc // na
    k, waves, z = dual_focal.shape
    u = focal_rows.shape[1]
    rows, cols = transmission.shape
    tile = min(512, rows)
    assert rows == cols and u <= rows and u == z, "tile shape"
    b = lambda *dims: pltpu.VMEM(dims, bf16)
    v = lambda *dims: pltpu.VMEM(dims, f32)
    scratch = dict(
        rh=b(waves, u, rows), rl=b(waves, u, rows), ch=b(waves, z, cols), cl=b(waves, z, cols), stage_sems=DMA((waves, 2)),
        ah=b(rows, cols), al=b(rows, cols), ext_v=v(rows, cols), dual_v=v(rows, cols), local=DMA((2,)),
        full=v(waves, nr, nc, k, z), part=v(waves, nr, nc, k, z), lh=b(u, cols), ll=b(u, cols), sh=b(tile, z), sl=b(tile, z),
        yh=b(u, z), yl=b(u, z), dual_r=v(2, 8, cols), dual_c=v(2, 8, rows), ext_r=v(2, 8, cols), ext_c=v(2, 8, rows),
        free=pltpu.SemaphoreType.REGULAR, gather=Gather.scratch(waves, nr, na, nb), scatter=Scatter.scratch(waves, nr, na, nb, k, z),
        halos=Halo.scratch(rows, cols) * (2 * ITERS), **Primal.scratch(rows, cols, nw, tile))
    ins = dict(
        y=(dual_focal, VMEM), dark=(dark_mask, VMEM), x=(transmission, ANY), dual=(dual_curvature, ANY), pupil=(pupil_mask, ANY),
        lyot=(lyot_mask, ANY), focal_rows=(focal_rows, ANY), focal_cols=(focal_cols, ANY))
    outs = dict(
        x_out=(shape(rows, cols), ANY), y_out=(shape(k, waves, z), VMEM), dual_out=(shape(rows, cols), ANY), x_mid=(shape(rows, cols), ANY))
    out = call(ins, outs, scratch)
    return out.x_out, out.y_out, out.dual_out


def solution(mesh):
    return jax.shard_map(
        per_device,
        mesh=mesh,
        in_specs=(
            P("row", "col"),
            P(("row", "col"), "wave", None),
            P("row", "col"),
            P("row", "col"),
            P("row", "col"),
            P(("row", "col"), "wave", None),
            P("wave", None, "row"),
            P("wave", None, "col"),
        ),
        out_specs=(P("row", "col"), P(("row", "col"), "wave", None), P("row", "col")),
        check_vma=False,
    )
```
